32 devices in a mesh: groups: 2 (over y), tile: 16 (over z, x, core).
Axes of the slice: x: 2, y: 2, z: 4, core: 2. Of those that a mesh axis runs over, the one named last changes fastest.
Arguments:
- level_map: int32 [16], replicated, may hold values from 0 to 7, as said below
- loc_lat: bfloat16 [256, 256], replicated, may hold values from -0.1875 to 0.1875
- loc_lon: bfloat16 [256, 256], replicated, may hold values from -0.1875 to 0.1875
- ens_perts: bfloat16 [32, 256, 256], P(('groups', 'tile')), parts along dimension 0, may hold values from -4 to 4
- ens_control: float32 [32, 256, 256], P(('groups', 'tile')), parts along dimension 0, may hold values from -6 to 6
- static_control: float32 [16, 256, 256], P('groups', 'tile'), parts along dimension 0, may hold values from -6 to 6
- static_scale: float32 [16, 256, 256], P('groups', 'tile'), parts along dimension 0, may hold values from 0.3 to 1.5
- coefs: float32 [4, 16, 256, 256], P(None, 'groups', 'tile'), parts along dimension 1, may hold values from 0.02 to 0.24
- obs_weight: float32 [3, 16, 256, 256], P(None, 'groups', 'tile'), parts along dimension 1, may hold values from 0.05 to 0.5
- innovation: float32 [3, 16, 256, 256], P(None, 'groups', 'tile'), parts along dimension 1, may hold values from -6 to 6
Outputs:
- ens_final: float32 [32, 256, 256], P(('groups', 'tile')), parts along dimension 0
- static_final: float32 [16, 256, 256], P('groups', 'tile'), parts along dimension 0
The draws below stay inside these ranges and needn't reach their ends.
There are 2 independent parts, one for each index of `groups`. The reference program is written for one: setup_inputs(seed, part) draws one part's arguments, and reference() takes and returns one part's arrays. A program takes and returns all parts, laid end to end along the dimension named above; an argument that names none is the same for every part. Nothing has to cross between parts.
Inputs may be any that keep to these rules, and one draw needn't show every extreme that they name: `level_map`: each of the 8 levels is named by exactly 2 entries.
All inputs are finite; a program needn't handle non-finite values.
Results may differ from the reference program's by a relative error of at most 0.0003.
Values sent between devices are 32-bit elements; how exact they have to be, the bound alone decides.
No kernel may reach another device: no remote copies, remote signals or barrier semaphores. Data moves between devices by JAX's collectives and lax.ppermute only.
A program may use at most 64 MiB of HBM per device.

```python
import math
import jax
import jax.numpy as jnp
from jax import lax

NLAT = 256
NLON = 256
LEV = 8
MEM_DEV = 1
STEPS = 3
ITERS = 1
GROUP_DEV = 2
MEMBERS = 2
BLOCKS = 16
N_TILE = 16


def draw_level_map(key, part):
    levels_sorted = jnp.repeat(jnp.arange(LEV, dtype=jnp.int32), GROUP_DEV)
    return jax.random.permutation(jax.random.fold_in(key, 7), levels_sorted)


def block_levels(key, dims, split, least, largest):
    level, own = 1.0, jax.random.fold_in(key, 6)
    for position, parts in split:
        draws = jnp.exp(jax.random.uniform(jax.random.fold_in(own, position), (parts,), jnp.float32, least / len(split), largest / len(split)))
        level = level * jnp.repeat(draws, dims[position] // parts).reshape([-1 if axis == position else 1 for axis in range(len(dims))])
    return level


def centred(rng, shape, width, reach, split=(), held_as=jnp.bfloat16):
    result = jax.random.normal(rng, shape, jnp.float32) * width
    if len(split) > 0:
        result = block_levels(rng, shape, split, -0.22, 0.18) * result
    return jnp.clip(result, min=-reach, max=reach).astype(held_as)


def setup_inputs(seed: int = 0, part: int = 0) -> dict:
    arg_keys = jax.random.split(jax.random.key(seed), 11)
    part_splits = jax.random.split(jax.random.fold_in(arg_keys[10], part), 11)
    return {
        "level_map": draw_level_map(jax.random.fold_in(arg_keys[10], 71), part),
        "loc_lat": centred(arg_keys[1], (NLAT, NLAT), (4 * NLAT) ** -0.5, 0.1875),
        "loc_lon": centred(arg_keys[2], (NLON, NLON), (4 * NLON) ** -0.5, 0.1875),
        "ens_perts": centred(part_splits[3], (BLOCKS, NLAT, NLON), (MEMBERS ** -0.5), 4.0, ((0, 16),)),
        "ens_control": centred(part_splits[4], (BLOCKS, NLAT, NLON), 1.0, 6.0, ((0, 16),), jnp.float32),
        "static_control": centred(part_splits[5], (LEV, NLAT, NLON), 1.0, 6.0, ((1, 16),), jnp.float32),
        "static_scale": jnp.clip(jnp.exp(math.log(1.5) - 1.60943787 * jax.random.uniform(part_splits[6], (LEV, NLAT, NLON), jnp.float32) ** block_levels(part_splits[6], (LEV, NLAT, NLON), ((1, 16),), -0.2, 0.2)), 0.3, 1.5),
        "coefs": jnp.clip(0.02 + 0.22 * jax.random.uniform(part_splits[7], (4, LEV, NLAT, NLON), jnp.float32) ** block_levels(part_splits[7], (4, LEV, NLAT, NLON), ((2, 16),), -0.2, 0.2), 0.02, 0.24),
        "obs_weight": jnp.clip(jnp.exp(math.log(0.5) - 2.3025851 * jax.random.uniform(part_splits[8], (STEPS, LEV, NLAT, NLON), jnp.float32) ** block_levels(part_splits[8], (STEPS, LEV, NLAT, NLON), ((2, 16),), -0.2, 0.2)), 0.05, 0.5),
        "innovation": centred(part_splits[9], (STEPS, LEV, NLAT, NLON), 1.0, 6.0, ((2, 16),), jnp.float32),
    }


step_size = 0.15


def rounded(values):
    return lax.optimization_barrier(values.astype(jnp.bfloat16)).astype(jnp.float32)


def forward_step(state, coeffs):
    padded = jnp.pad(state, ((0, 0), (1, 1), (0, 0)))
    north_rows = padded[:, 2:]
    south_rows = padded[:, :-2]
    east_cells = jnp.roll(state, -1, 2)
    west_cells = jnp.roll(state, 1, 2)
    return state + coeffs[0] * (north_rows - state) + coeffs[1] * (south_rows - state) + coeffs[2] * (east_cells - state) + coeffs[3] * (west_cells - state)


def adjoint_step(adjoint, coeffs):
    coef_sum = coeffs[0] + coeffs[1] + coeffs[2] + coeffs[3]
    north_flux = jnp.pad(coeffs[0] * adjoint, ((0, 0), (1, 1), (0, 0)))[:, :-2]
    south_flux = jnp.pad(coeffs[1] * adjoint, ((0, 0), (1, 1), (0, 0)))[:, 2:]
    return (1.0 - coef_sum) * adjoint + north_flux + south_flux + jnp.roll(coeffs[2] * adjoint, 1, 2) + jnp.roll(coeffs[3] * adjoint, -1, 2)


def window_gradient(total_incr, coefs, obs_weight, innovation):
    state = total_incr
    weighted = []
    for section in range(STEPS):
        state = forward_step(state, coefs)
        weighted.append(obs_weight[section] * (state - innovation[section]))
    adjoint = weighted[STEPS - 1]
    for section in range(STEPS - 2, -1, -1):
        adjoint = adjoint_step(adjoint, coefs) + weighted[section]
    return adjoint_step(adjoint, coefs)


def reference(level_map, loc_lat, loc_lon, ens_perts, ens_control, static_control, static_scale, coefs, obs_weight, innovation):
    lat_matrix = loc_lat.astype(jnp.float32)
    lon_matrix = loc_lon.astype(jnp.float32)
    perts = ens_perts.reshape(N_TILE, MEM_DEV, NLAT, NLON)
    level_onehot = (level_map[:, None] == jnp.arange(LEV, dtype=jnp.int32)[None, :]).astype(jnp.float32)

    def member_sum(operands):
        members, control = operands
        lat_smoothed = rounded(jnp.einsum('ij,bjk->bik', lat_matrix, rounded(control)))
        member_field = jnp.einsum('bij,kj->bik', lat_smoothed, lon_matrix)
        return jnp.sum(members.astype(jnp.float32) * member_field, axis=0)

    def member_update(operands):
        members, control, grad_field = operands
        weighted_grad = rounded(members.astype(jnp.float32) * grad_field[None])
        adjoint_lat = rounded(jnp.einsum('ji,bjk->bik', lat_matrix, weighted_grad))
        member_grad = jnp.einsum('bij,jk->bik', adjoint_lat, lon_matrix)
        return control - step_size * (control + member_grad)

    control = ens_control.reshape(N_TILE, MEM_DEV, NLAT, NLON)
    for sweep in range(ITERS):
        partials = lax.map(member_sum, (perts, control))
        ens_incr = jnp.einsum('dl,dij->lij', level_onehot, partials, precision=lax.Precision.HIGHEST)
        total_incr = static_scale * static_control + ens_incr
        gradient = window_gradient(total_incr, coefs, obs_weight, innovation)
        static_control = static_control - step_size * (static_control + static_scale * gradient)
        grad_fields = jnp.take(gradient, level_map, axis=0)
        control = lax.map(member_update, (perts, control, grad_fields))
    return control.reshape(BLOCKS, NLAT, NLON), static_control
```

```python
import jax
import jax.numpy as jnp
from jax import lax
from jax.sharding import PartitionSpec as P

STEPS = 3


step_size = 0.15


def extended(block, sides, width):
    for axis, dim in sides:
        count = lax.axis_size(axis)
        forward = [(i, i + 1) for i in range(count - 1)]
        backward = [(target, source) for source, target in forward]
        low = lax.ppermute(
            lax.slice_in_dim(block, block.shape[dim] - width, None, axis=dim), axis, forward
        )
        high = lax.ppermute(lax.slice_in_dim(block, 0, width, axis=dim), axis, backward)
        block = jnp.concatenate([low, block, high], axis=dim)
    return block


def forward_step(state, coeffs):
    padded = extended(state, (("tile", 1),), 1)
    north_rows = padded[:, 2:]
    south_rows = padded[:, :-2]
    east_cells = jnp.roll(state, -1, 2)
    west_cells = jnp.roll(state, 1, 2)
    return (
        state
        + coeffs[0] * (north_rows - state)
        + coeffs[1] * (south_rows - state)
        + coeffs[2] * (east_cells - state)
        + coeffs[3] * (west_cells - state)
    )


def adjoint_step(adjoint, coeffs):
    coef_sum = coeffs[0] + coeffs[1] + coeffs[2] + coeffs[3]
    fluxes = jnp.stack([coeffs[0] * adjoint, coeffs[1] * adjoint])
    padded = extended(fluxes, (("tile", 2),), 1)
    north_flux = padded[0][:, :-2]
    south_flux = padded[1][:, 2:]
    return (
        (1.0 - coef_sum) * adjoint
        + north_flux
        + south_flux
        + jnp.roll(coeffs[2] * adjoint, 1, 2)
        + jnp.roll(coeffs[3] * adjoint, -1, 2)
    )


def window_gradient(total_incr, coefs, obs_weight, innovation):
    state = total_incr
    weighted = []
    for section in range(STEPS):
        state = forward_step(state, coefs)
        weighted.append(obs_weight[section] * (state - innovation[section]))
    adjoint = weighted[STEPS - 1]
    for section in range(STEPS - 2, -1, -1):
        adjoint = adjoint_step(adjoint, coefs) + weighted[section]
    return adjoint_step(adjoint, coefs)


def local(
    level_map,
    loc_lat,
    loc_lon,
    ens_perts,
    ens_control,
    static_control,
    static_scale,
    coefs,
    obs_weight,
    innovation,
):
    tile_count = lax.axis_size("tile")
    levels = static_control.shape[0]
    level_ids = jnp.arange(levels, dtype=jnp.int32)
    level_onehot = (level_map[:, None] == level_ids[None, :]).astype(jnp.float32)
    control = ens_control
    lat_smoothed = jnp.einsum(
        "ij,bjk->bik", loc_lat, control.astype(jnp.bfloat16), preferred_element_type=jnp.float32
    ).astype(jnp.bfloat16)
    member_field = jnp.einsum(
        "bij,kj->bik", lat_smoothed, loc_lon, preferred_element_type=jnp.float32
    )
    partial_value = jnp.sum(ens_perts.astype(jnp.float32) * member_field, axis=0)
    pieces = partial_value.reshape(tile_count, -1, partial_value.shape[1])
    received = lax.all_to_all(pieces, "tile", split_axis=0, concat_axis=0, tiled=True)
    ens_incr = jnp.einsum("dl,dij->lij", level_onehot, received, precision=lax.Precision.HIGHEST)
    total_incr = static_scale * static_control + ens_incr
    gradient = window_gradient(total_incr, coefs, obs_weight, innovation)
    static_control = static_control - step_size * (static_control + static_scale * gradient)
    outgoing = jnp.take(gradient, level_map, axis=0)
    incoming = lax.all_to_all(outgoing, "tile", split_axis=0, concat_axis=0, tiled=True)
    grad_field = incoming.reshape(-1, incoming.shape[2])
    weighted_grad = (ens_perts.astype(jnp.float32) * grad_field[None]).astype(jnp.bfloat16)
    adjoint_lat = jnp.einsum(
        "ji,bjk->bik", loc_lat, weighted_grad, preferred_element_type=jnp.float32
    ).astype(jnp.bfloat16)
    member_grad = jnp.einsum(
        "bij,jk->bik", adjoint_lat, loc_lon, preferred_element_type=jnp.float32
    )
    control = control - step_size * (control + member_grad)
    return (control, static_control)


def solution(mesh):
    in_specs = (
        P(),
        P(),
        P(),
        P(("groups", "tile"), None, None),
        P(("groups", "tile"), None, None),
        P("groups", "tile", None),
        P("groups", "tile", None),
        P(None, "groups", "tile", None),
        P(None, "groups", "tile", None),
        P(None, "groups", "tile", None),
    )
    out_specs = (P(("groups", "tile"), None, None), P("groups", "tile", None))
    return jax.shard_map(local, mesh=mesh, in_specs=in_specs, out_specs=out_specs, check_vma=False)
```

```python
import jax
import jax.numpy as jnp
from jax import lax
from jax.experimental import pallas as pl
from jax.experimental.pallas import tpu as pltpu
from jax.sharding import PartitionSpec as P

STEPS = 3
LANES = 128
SUB = 8
STEP_SIZE = 0.15

HALO = 2 * STEPS
COEF_ROWS = HALO - 1


def weight_rows(section):
    return section + 1


def packed_fields():
    fields = [("coefs", k, COEF_ROWS) for k in range(4)]
    for section in range(STEPS):
        fields.append(("obs_weight", section, weight_rows(section)))
        fields.append(("innovation", section, weight_rows(section)))
    return fields


PACKED_ROWS = sum(rows for _, _, rows in packed_fields())
HALO_ROWS = -(-(SUB + PACKED_ROWS) // SUB) * SUB


def vmem(count):
    return [pl.BlockSpec(memory_space=pltpu.VMEM)] * count


def member_sum_kernel(tiles, lat_ref, lon_ref, perts_ref, control_ref, out_ref, padded_ref):
    blocks, nlat, nlon = control_ref.shape
    rows = nlat // tiles
    tall = rows + 2 * HALO
    total = None
    for b in range(blocks):
        smoothed = jnp.dot(
            lat_ref[...], control_ref[b].astype(jnp.bfloat16), preferred_element_type=jnp.float32
        ).astype(jnp.bfloat16)
        field = lax.dot_general(
            smoothed, lon_ref[...], (((1,), (1,)), ((), ())), preferred_element_type=jnp.float32
        )
        term = perts_ref[b].astype(jnp.float32) * field
        total = term if total is None else total + term
    edge = jnp.zeros((SUB, nlon), jnp.float32)
    padded_ref[0:SUB, :] = edge
    padded_ref[SUB + nlat : 2 * SUB + nlat, :] = edge
    padded_ref[SUB : SUB + nlat, :] = total
    for e in range(tiles):
        start = SUB + e * rows - HALO
        for h in range(nlon // LANES):
            out_ref[e, h * tall : (h + 1) * tall, :] = padded_ref[
                start : start + tall, h * LANES : (h + 1) * LANES
            ]


def pack_kernel(control_ref, scale_ref, coefs_ref, weight_ref, innov_ref, up_ref, down_ref):
    refs = {"coefs": coefs_ref, "obs_weight": weight_ref, "innovation": innov_ref}
    rows = control_ref.shape[1]

    def level(l, carry):
        scale, control = scale_ref.at[l], control_ref.at[l]
        last, first = slice(rows - SUB, rows), slice(0, SUB)
        up_ref[l, 0:SUB, :] = scale[last, :] * control[last, :]
        down_ref[l, HALO_ROWS - SUB : HALO_ROWS, :] = scale[first, :] * control[first, :]
        up_at, down_at = SUB, 0
        for name, k, count in packed_fields():
            field = refs[name].at[k, l]
            up_ref[l, up_at : up_at + count, :] = field[rows - count : rows, :]
            down_ref[l, down_at : down_at + count, :] = field[0:count, :]
            up_at, down_at = up_at + count, down_at + count
        return carry

    lax.fori_loop(0, control_ref.shape[0], level, 0)


def window_kernel(
    level_ref,
    received_ref,
    low_ref,
    high_ref,
    control_ref,
    scale_ref,
    coefs_ref,
    weight_ref,
    innov_ref,
    send_ref,
    grad_ref,
    sums_ref,
):
    tiles = received_ref.shape[0]
    levels, rows, nlon = control_ref.shape
    tall = rows + 2 * HALO
    ext = rows + 2 * SUB
    halves = nlon // LANES
    packed = halves * tall
    refs = {"coefs": coefs_ref, "obs_weight": weight_ref, "innovation": innov_ref}

    sums_ref[...] = jnp.zeros_like(sums_ref)
    for d in range(tiles):
        at = level_ref[d]
        sums_ref[at, SUB : SUB + packed, :] += received_ref[d]

    def level(l, carry):
        parts = []
        for h in range(halves):
            start = SUB + h * tall - (SUB - HALO)
            parts.append(sums_ref[l, start : start + ext, :])
        ens = jnp.concatenate(parts, axis=1)
        static = jnp.concatenate(
            [
                low_ref[l, 0:SUB, :],
                scale_ref[l] * control_ref[l],
                high_ref[l, HALO_ROWS - SUB : HALO_ROWS, :],
            ],
            axis=0,
        )
        state = static + ens
        fields = {}
        low_at, high_at = SUB, 0
        for name, k, count in packed_fields():
            low_at += count
            fields[name, k] = jnp.concatenate(
                [
                    low_ref[l, low_at - SUB : low_at, :],
                    refs[name][k, l],
                    high_ref[l, high_at : high_at + SUB, :],
                ],
                axis=0,
            )
            high_at += count
        c0, c1, c2, c3 = (fields["coefs", k] for k in range(4))
        rest = 1.0 - (c0 + c1 + c2 + c3)
        weighted = []
        for section in range(STEPS):
            state = (
                rest * state
                + c0 * pltpu.roll(state, ext - 1, 0)
                + c1 * pltpu.roll(state, 1, 0)
                + c2 * pltpu.roll(state, nlon - 1, 1)
                + c3 * pltpu.roll(state, 1, 1)
            )
            weighted.append(
                fields["obs_weight", section] * (state - fields["innovation", section])
            )
        adjoint = weighted[STEPS - 1]
        for section in range(STEPS - 2, -2, -1):
            adjoint = (
                rest * adjoint
                + pltpu.roll(c0 * adjoint, 1, 0)
                + pltpu.roll(c1 * adjoint, ext - 1, 0)
                + pltpu.roll(c2 * adjoint, 1, 1)
                + pltpu.roll(c3 * adjoint, nlon - 1, 1)
            )
            if section >= 0:
                adjoint = adjoint + weighted[section]
        grad_ref[l] = adjoint[SUB : SUB + rows, :]
        return carry

    lax.fori_loop(0, levels, level, 0)
    for e in range(tiles):
        send_ref[e] = grad_ref[level_ref[e]]


def member_update_kernel(lat_ref, lon_ref, perts_ref, grad_ref, control_ref, out_ref):
    for b in range(control_ref.shape[0]):
        weighted = (perts_ref[b].astype(jnp.float32) * grad_ref[...]).astype(jnp.bfloat16)
        adjoint_lat = lax.dot_general(
            lat_ref[...], weighted, (((0,), (0,)), ((), ())), preferred_element_type=jnp.float32
        ).astype(jnp.bfloat16)
        member_grad = jnp.dot(adjoint_lat, lon_ref[...], preferred_element_type=jnp.float32)
        control = control_ref[b]
        out_ref[b] = control - STEP_SIZE * (control + member_grad)


def tall_local(
    level_map, loc_lat, loc_lon, ens_perts, ens_control,
    static_control, static_scale, coefs, obs_weight, innovation,
):
    tiles = lax.axis_size("tile")
    levels, rows, nlon = static_control.shape
    nlat = ens_control.shape[1]
    tall = rows + 2 * HALO
    packed = tall * (nlon // LANES)
    pieces = pl.pallas_call(
        lambda *refs: member_sum_kernel(tiles, *refs),
        out_shape=jax.ShapeDtypeStruct((tiles, packed, LANES), jnp.float32),
        in_specs=vmem(4),
        out_specs=pl.BlockSpec(memory_space=pltpu.VMEM),
        scratch_shapes=[pltpu.VMEM((nlat + 2 * SUB, nlon), jnp.float32)],
        name="member_sum",
    )(loc_lat, loc_lon, ens_perts, ens_control)
    received = lax.all_to_all(pieces, "tile", split_axis=0, concat_axis=0, tiled=True)

    halo = jax.ShapeDtypeStruct((levels, HALO_ROWS, nlon), jnp.float32)
    up, down = pl.pallas_call(
        pack_kernel,
        out_shape=(halo, halo),
        in_specs=vmem(5),
        out_specs=tuple(vmem(2)),
        name="pack",
    )(static_control, static_scale, coefs, obs_weight, innovation)
    forward = [(i, i + 1) for i in range(tiles - 1)]
    backward = [(target, source) for source, target in forward]
    low = lax.ppermute(up, "tile", forward)
    high = lax.ppermute(down, "tile", backward)

    send, gradient = pl.pallas_call(
        window_kernel,
        out_shape=(
            jax.ShapeDtypeStruct((tiles, rows, nlon), jnp.float32),
            jax.ShapeDtypeStruct((levels, rows, nlon), jnp.float32),
        ),
        in_specs=[pl.BlockSpec(memory_space=pltpu.SMEM)] + vmem(8),
        out_specs=tuple(vmem(2)),
        scratch_shapes=[pltpu.VMEM((levels, packed + 2 * SUB, LANES), jnp.float32)],
        name="window",
    )(level_map, received, low, high, static_control, static_scale, coefs, obs_weight, innovation)
    incoming = lax.all_to_all(send, "tile", split_axis=0, concat_axis=0, tiled=True)
    static_final = static_control - STEP_SIZE * (static_control + static_scale * gradient)

    ens_final = pl.pallas_call(
        member_update_kernel,
        out_shape=jax.ShapeDtypeStruct(ens_control.shape, jnp.float32),
        in_specs=vmem(5),
        out_specs=pl.BlockSpec(memory_space=pltpu.VMEM),
        name="member_update",
    )(loc_lat, loc_lon, ens_perts, incoming.reshape(nlat, nlon), ens_control)
    return ens_final, static_final


def exchanged(block, axis):
    count = lax.axis_size("tile")
    forward = [(i, i + 1) for i in range(count - 1)]
    backward = [(target, source) for source, target in forward]
    last = block.shape[axis] - 1
    low = lax.ppermute(lax.slice_in_dim(block, last, last + 1, axis=axis), "tile", forward)
    high = lax.ppermute(lax.slice_in_dim(block, 0, 1, axis=axis), "tile", backward)
    return jnp.concatenate([low, block, high], axis=axis)


def forward_step(state, coeffs):
    padded = exchanged(state, 1)
    return (
        state
        + coeffs[0] * (padded[:, 2:] - state)
        + coeffs[1] * (padded[:, :-2] - state)
        + coeffs[2] * (jnp.roll(state, -1, 2) - state)
        + coeffs[3] * (jnp.roll(state, 1, 2) - state)
    )


def adjoint_step(adjoint, coeffs):
    coef_sum = coeffs[0] + coeffs[1] + coeffs[2] + coeffs[3]
    padded = exchanged(jnp.stack([coeffs[0] * adjoint, coeffs[1] * adjoint]), 2)
    return (
        (1.0 - coef_sum) * adjoint
        + padded[0][:, :-2]
        + padded[1][:, 2:]
        + jnp.roll(coeffs[2] * adjoint, 1, 2)
        + jnp.roll(coeffs[3] * adjoint, -1, 2)
    )


def any_local(
    level_map, loc_lat, loc_lon, ens_perts, ens_control,
    static_control, static_scale, coefs, obs_weight, innovation,
):
    tiles = lax.axis_size("tile")
    level_ids = jnp.arange(static_control.shape[0], dtype=jnp.int32)
    level_onehot = (level_map[:, None] == level_ids[None, :]).astype(jnp.float32)
    lat_smoothed = jnp.einsum(
        "ij,bjk->bik", loc_lat, ens_control.astype(jnp.bfloat16),
        preferred_element_type=jnp.float32,
    ).astype(jnp.bfloat16)
    member_field = jnp.einsum(
        "bij,kj->bik", lat_smoothed, loc_lon, preferred_element_type=jnp.float32
    )
    partial_value = jnp.sum(ens_perts.astype(jnp.float32) * member_field, axis=0)
    pieces = partial_value.reshape(tiles, -1, partial_value.shape[1])
    received = lax.all_to_all(pieces, "tile", split_axis=0, concat_axis=0, tiled=True)
    ens_incr = jnp.einsum("dl,dij->lij", level_onehot, received, precision=lax.Precision.HIGHEST)
    state = static_scale * static_control + ens_incr
    weighted = []
    for section in range(STEPS):
        state = forward_step(state, coefs)
        weighted.append(obs_weight[section] * (state - innovation[section]))
    adjoint = weighted[STEPS - 1]
    for section in range(STEPS - 2, -1, -1):
        adjoint = adjoint_step(adjoint, coefs) + weighted[section]
    gradient = adjoint_step(adjoint, coefs)
    static_final = static_control - STEP_SIZE * (static_control + static_scale * gradient)
    outgoing = jnp.take(gradient, level_map, axis=0)
    incoming = lax.all_to_all(outgoing, "tile", split_axis=0, concat_axis=0, tiled=True)
    grad_field = incoming.reshape(-1, incoming.shape[2])
    weighted_grad = (ens_perts.astype(jnp.float32) * grad_field[None]).astype(jnp.bfloat16)
    adjoint_lat = jnp.einsum(
        "ji,bjk->bik", loc_lat, weighted_grad, preferred_element_type=jnp.float32
    ).astype(jnp.bfloat16)
    member_grad = jnp.einsum("bij,jk->bik", adjoint_lat, loc_lon, preferred_element_type=jnp.float32)
    return ens_control - STEP_SIZE * (ens_control + member_grad), static_final


def local(*args):
    _, rows, nlon = args[5].shape
    whole_tiles = rows % SUB == 0 and nlon % LANES == 0
    return (tall_local if whole_tiles else any_local)(*args)


def solution(mesh):
    in_specs = (
        P(),
        P(),
        P(),
        P(("groups", "tile"), None, None),
        P(("groups", "tile"), None, None),
        P("groups", "tile", None),
        P("groups", "tile", None),
        P(None, "groups", "tile", None),
        P(None, "groups", "tile", None),
        P(None, "groups", "tile", None),
    )
    out_specs = (P(("groups", "tile"), None, None), P("groups", "tile", None))
    return jax.shard_map(local, mesh=mesh, in_specs=in_specs, out_specs=out_specs, check_vma=False)
```

```python
import jax
import jax.numpy as jnp
from jax import lax
from jax.experimental import pallas as pl
from jax.experimental.pallas import tpu as pltpu
from jax.sharding import PartitionSpec as P

STEPS = 3
LANES = 128
SUB = 8
STEP_SIZE = 0.15
GROUP = 4

SPILL = 2
HALO = 2 * STEPS - SPILL


def packed_fields():
    fields = [("static", 0, HALO)]
    fields += [("coefs", k, HALO - 1) for k in range(4)]
    for section in range(SPILL, STEPS):
        fields += [(name, section, section + 1 - SPILL) for name in ("obs_weight", "innovation")]
    return fields


LEVEL_ROWS = sum(rows for _, _, rows in packed_fields())
PACKED = GROUP * LEVEL_ROWS


def vmem(count):
    return [pl.BlockSpec(memory_space=pltpu.VMEM)] * count


def params(mebibytes):
    return pltpu.CompilerParams(vmem_limit_bytes=mebibytes << 20)


def sublane(shape):
    return lax.broadcasted_iota(jnp.int32, shape, 0)


def member_sum_kernel(tiles, lat_ref, lon_ref, perts_ref, control_ref, out_ref):
    blocks, nlat, nlon = control_ref.shape
    rows = nlat // tiles
    halves = nlon // LANES
    total = None
    for b in range(blocks):
        smoothed = jnp.dot(
            lat_ref[...], control_ref[b].astype(jnp.bfloat16), preferred_element_type=jnp.float32
        ).astype(jnp.bfloat16)
        field = lax.dot_general(
            smoothed, lon_ref[...], (((1,), (1,)), ((), ())), preferred_element_type=jnp.float32
        )
        term = perts_ref[b].astype(jnp.float32) * field
        total = term if total is None else total + term
    first = sublane((SUB, LANES)) < HALO
    edge = jnp.zeros((SUB, LANES), jnp.float32)
    for e in range(tiles):
        for h in range(halves):
            lanes = slice(h * LANES, (h + 1) * LANES)
            start, end = e * rows, (e + 1) * rows
            above = total[end : end + SUB, lanes] if end < nlat else edge
            below = total[start - SUB : start, lanes] if start > 0 else edge
            out_ref[e, h * rows : (h + 1) * rows, :] = total[start:end, lanes]
            at = halves * rows + h * SUB
            out_ref[e, at : at + SUB, :] = jnp.where(first, above, below)


def pack_kernel(control_ref, scale_ref, coefs_ref, weight_ref, innov_ref, up_ref, down_ref):
    refs = {"coefs": coefs_ref, "obs_weight": weight_ref, "innovation": innov_ref}
    levels, rows, _ = control_ref.shape
    for l in range(levels):
        at = l % GROUP * LEVEL_ROWS
        for name, k, count in packed_fields():
            last, first = slice(rows - count, rows), slice(0, count)
            if name == "static":
                high = scale_ref[l, last, :] * control_ref[l, last, :]
                low = scale_ref[l, first, :] * control_ref[l, first, :]
            else:
                high, low = refs[name][k, l, last, :], refs[name][k, l, first, :]
            up_ref[l // GROUP, at : at + count, :] = high
            down_ref[l // GROUP, at : at + count, :] = low
            at += count


def window_kernel(
    level_ref,
    received_ref,
    low_ref,
    high_ref,
    control_ref,
    scale_ref,
    coefs_ref,
    weight_ref,
    innov_ref,
    send_ref,
    grad_ref,
    up_ref,
    down_ref,
    sums_ref,
):
    tiles = received_ref.shape[0]
    levels, rows, nlon = control_ref.shape
    ext = rows + 2 * SUB
    halves = nlon // LANES
    refs = {"coefs": coefs_ref, "obs_weight": weight_ref, "innovation": innov_ref}
    own = slice(SUB, SUB + rows)

    sums_ref[...] = jnp.zeros_like(sums_ref)
    for d in range(tiles):
        sums_ref[level_ref[d]] += received_ref[d]

    row = sublane((SUB, nlon))
    mine = (sublane((ext, nlon)) >= SUB) & (sublane((ext, nlon)) < SUB + rows)

    def low_rows(g, at, count):
        start = max(at + count - SUB, 0)
        block = low_ref[g, start : start + SUB, :]
        shift = SUB - (at + count - start)
        return pltpu.roll(block, shift, 0) if shift else block

    def high_rows(g, at):
        start = min(at, PACKED - SUB)
        block = high_ref[g, start : start + SUB, :]
        return pltpu.roll(block, SUB - (at - start), 0) if at > start else block

    def level(g, i):
        l = g * GROUP + i
        fields = {}
        at = i * LEVEL_ROWS
        for name, k, count in packed_fields():
            centre = scale_ref[l] * control_ref[l] if name == "static" else refs[name][k, l]
            fields[name, k] = jnp.concatenate(
                [low_rows(g, at, count), centre, high_rows(g, at)], axis=0
            )
            at += count
        c0, c1, c2, c3 = (fields["coefs", k] for k in range(4))
        rest = 1.0 - (c0 + c1 + c2 + c3)

        sums = []
        for h in range(halves):
            edge = sums_ref[l, halves * rows + h * SUB : halves * rows + (h + 1) * SUB, :]
            sums.append(
                jnp.concatenate([edge, sums_ref[l, h * rows : (h + 1) * rows, :], edge], axis=0)
            )
        state = fields["static", 0] + jnp.concatenate(sums, axis=1)
        weighted = []
        for section in range(STEPS):
            state = (
                rest * state
                + c0 * pltpu.roll(state, ext - 1, 0)
                + c1 * pltpu.roll(state, 1, 0)
                + c2 * pltpu.roll(state, nlon - 1, 1)
                + c3 * pltpu.roll(state, 1, 1)
            )
            if section < SPILL:
                value = weight_ref[section, l] * (state[own] - innov_ref[section, l])
                edge = jnp.zeros((SUB, nlon), jnp.float32)
                value = jnp.concatenate([edge, value, edge], axis=0)
            else:
                value = fields["obs_weight", section] * (state - fields["innovation", section])
            weighted.append(value)
        adjoint = weighted[STEPS - 1]
        for left in range(STEPS - 1, -1, -1):
            if left + 1 == SPILL:
                adjoint = jnp.where(mine, adjoint, 0.0)
            adjoint = (
                rest * adjoint
                + pltpu.roll(c0 * adjoint, 1, 0)
                + pltpu.roll(c1 * adjoint, ext - 1, 0)
                + pltpu.roll(c2 * adjoint, 1, 1)
                + pltpu.roll(c3 * adjoint, nlon - 1, 1)
            )
            if left > 0:
                adjoint = adjoint + weighted[left - 1]
        grad_ref[l, 0:rows, :] = adjoint[own]
        spilled = jnp.where(row < SPILL, adjoint[SUB + rows :], adjoint[:SUB])
        grad_ref[l, rows : rows + SUB, :] = spilled
        up_ref[g, i * SPILL : (i + 1) * SPILL, :] = spilled[0:SPILL]
        down_ref[g, i * SPILL : (i + 1) * SPILL, :] = spilled[SUB - SPILL :]

    def group(g, carry):
        for i in range(GROUP):
            level(g, i)
        return carry

    lax.fori_loop(0, levels // GROUP, group, 0)
    half_row = sublane((SUB, LANES))
    for e in range(tiles):
        at = level_ref[e]
        spilled = None
        for h in range(halves):
            lanes = slice(h * LANES, (h + 1) * LANES)
            send_ref[e, h * rows : (h + 1) * rows, :] = grad_ref[at, 0:rows, lanes]
            block = grad_ref[at, rows : rows + SUB, lanes]
            if h % 2 == 0:
                spilled = block
            if h % 2 == 1 or h == halves - 1:
                if h % 2 == 1:
                    spilled = jnp.where(half_row < SPILL, spilled, jnp.where(
                        half_row >= SUB - SPILL, spilled, jnp.where(
                            half_row < 2 * SPILL, pltpu.roll(block, SPILL, 0),
                            pltpu.roll(block, SUB - SPILL, 0))))
                start = halves * rows + h // 2 * SUB
                send_ref[e, start : start + SUB, :] = spilled


def member_update_kernel(
    lat_ref,
    lon_ref,
    perts_ref,
    incoming_ref,
    control_ref,
    low_ref,
    high_ref,
    tile_grad_ref,
    static_ref,
    scale_ref,
    out_ref,
    static_out_ref,
    field_ref,
):
    tiles = incoming_ref.shape[0]
    blocks, nlat, nlon = control_ref.shape
    rows = nlat // tiles
    halves = nlon // LANES
    half_row = sublane((SUB, LANES))
    for h in range(halves):
        lanes = slice(h * LANES, (h + 1) * LANES)
        start = halves * rows + h // 2 * SUB
        place = h % 2 * SPILL

        def spill(s, above):
            block = incoming_ref[s, start : start + SUB, :]
            if place:
                block = pltpu.roll(block, SUB - place if above else place, 0)
            keep = half_row < SPILL if above else half_row >= SUB - SPILL
            return jnp.where(keep, block, 0.0)

        for s in range(tiles):
            piece = incoming_ref[s, h * rows : (h + 1) * rows, :]
            parts = [piece[t * SUB : (t + 1) * SUB] for t in range(rows // SUB)]
            if s > 0:
                parts[0] = parts[0] + spill(s - 1, True)
            if s < tiles - 1:
                parts[-1] = parts[-1] + spill(s + 1, False)
            field_ref[s * rows : (s + 1) * rows, lanes] = jnp.concatenate(parts, axis=0)
    for b in range(blocks):
        weighted = (perts_ref[b].astype(jnp.float32) * field_ref[...]).astype(jnp.bfloat16)
        adjoint_lat = lax.dot_general(
            lat_ref[...], weighted, (((0,), (0,)), ((), ())), preferred_element_type=jnp.float32
        ).astype(jnp.bfloat16)
        member_grad = jnp.dot(adjoint_lat, lon_ref[...], preferred_element_type=jnp.float32)
        control = control_ref[b]
        out_ref[b] = control - STEP_SIZE * (control + member_grad)

    row = sublane((SUB, nlon))
    for l in range(static_ref.shape[0]):
        at = l % GROUP * SPILL
        block = low_ref[l // GROUP, 0:SUB, :]
        above = jnp.where(row < SPILL, pltpu.roll(block, SUB - at, 0) if at else block, 0.0)
        block = high_ref[l // GROUP, 0:SUB, :]
        shift = (SUB - SPILL - at) % SUB
        below = jnp.where(
            row >= SUB - SPILL, pltpu.roll(block, shift, 0) if shift else block, 0.0
        )
        parts = [tile_grad_ref[l, t * SUB : (t + 1) * SUB, :] for t in range(rows // SUB)]
        parts[0] = parts[0] + above
        parts[-1] = parts[-1] + below
        gradient = jnp.concatenate(parts, axis=0)
        static = static_ref[l]
        static_out_ref[l] = static - STEP_SIZE * (static + scale_ref[l] * gradient)


def whole_local(
    level_map, loc_lat, loc_lon, ens_perts, ens_control,
    static_control, static_scale, coefs, obs_weight, innovation,
):
    tiles = lax.axis_size("tile")
    levels, rows, nlon = static_control.shape
    halves = nlon // LANES
    forward = [(i, i + 1) for i in range(tiles - 1)]
    backward = [(target, source) for source, target in forward]

    def array(*shape):
        return jax.ShapeDtypeStruct(shape, jnp.float32)

    first_shape = (tiles, halves * (rows + SUB), LANES)
    pieces = pl.pallas_call(
        lambda *refs: member_sum_kernel(tiles, *refs),
        out_shape=array(*first_shape),
        in_specs=vmem(4),
        out_specs=vmem(1)[0],
        name="member_sum",
    )(loc_lat, loc_lon, ens_perts, ens_control)
    received = lax.all_to_all(pieces, "tile", split_axis=0, concat_axis=0, tiled=True)

    packed = array(levels // GROUP, PACKED, nlon)
    up, down = pl.pallas_call(
        pack_kernel,
        out_shape=(packed, packed),
        in_specs=vmem(5),
        out_specs=tuple(vmem(2)),
        compiler_params=params(8),
        name="pack",
    )(static_control, static_scale, coefs, obs_weight, innovation)
    low = lax.ppermute(up, "tile", forward)
    high = lax.ppermute(down, "tile", backward)

    spilled = array(levels // GROUP, GROUP * SPILL, nlon)
    send, tile_grad, up, down = pl.pallas_call(
        window_kernel,
        out_shape=(
            array(tiles, halves * rows + -(-halves // 2) * SUB, LANES),
            array(levels, rows + SUB, nlon),
            spilled,
            spilled,
        ),
        in_specs=[pl.BlockSpec(memory_space=pltpu.SMEM)] + vmem(8),
        out_specs=tuple(vmem(4)),
        scratch_shapes=[pltpu.VMEM((levels,) + first_shape[1:], jnp.float32)],
        compiler_params=params(8),
        name="window",
    )(level_map, received, low, high, static_control, static_scale, coefs, obs_weight, innovation)
    incoming = lax.all_to_all(send, "tile", split_axis=0, concat_axis=0, tiled=True)
    low = lax.ppermute(up, "tile", forward)
    high = lax.ppermute(down, "tile", backward)

    return pl.pallas_call(
        member_update_kernel,
        out_shape=(array(*ens_control.shape), array(*static_control.shape)),
        in_specs=vmem(10),
        out_specs=tuple(vmem(2)),
        scratch_shapes=[pltpu.VMEM(ens_control.shape[1:], jnp.float32)],
        compiler_params=params(8),
        name="member_update",
    )(
        loc_lat, loc_lon, ens_perts, incoming, ens_control,
        low, high, tile_grad, static_control, static_scale,
    )


def exchanged(block, axis):
    count = lax.axis_size("tile")
    forward = [(i, i + 1) for i in range(count - 1)]
    backward = [(target, source) for source, target in forward]
    last = block.shape[axis] - 1
    low = lax.ppermute(lax.slice_in_dim(block, last, last + 1, axis=axis), "tile", forward)
    high = lax.ppermute(lax.slice_in_dim(block, 0, 1, axis=axis), "tile", backward)
    return jnp.concatenate([low, block, high], axis=axis)


def forward_step(state, coeffs):
    padded = exchanged(state, 1)
    return (
        state
        + coeffs[0] * (padded[:, 2:] - state)
        + coeffs[1] * (padded[:, :-2] - state)
        + coeffs[2] * (jnp.roll(state, -1, 2) - state)
        + coeffs[3] * (jnp.roll(state, 1, 2) - state)
    )


def adjoint_step(adjoint, coeffs):
    coef_sum = coeffs[0] + coeffs[1] + coeffs[2] + coeffs[3]
    padded = exchanged(jnp.stack([coeffs[0] * adjoint, coeffs[1] * adjoint]), 2)
    return (
        (1.0 - coef_sum) * adjoint
        + padded[0][:, :-2]
        + padded[1][:, 2:]
        + jnp.roll(coeffs[2] * adjoint, 1, 2)
        + jnp.roll(coeffs[3] * adjoint, -1, 2)
    )


def any_local(
    level_map, loc_lat, loc_lon, ens_perts, ens_control,
    static_control, static_scale, coefs, obs_weight, innovation,
):
    tiles = lax.axis_size("tile")
    level_ids = jnp.arange(static_control.shape[0], dtype=jnp.int32)
    level_onehot = (level_map[:, None] == level_ids[None, :]).astype(jnp.float32)
    lat_smoothed = jnp.einsum(
        "ij,bjk->bik", loc_lat, ens_control.astype(jnp.bfloat16),
        preferred_element_type=jnp.float32,
    ).astype(jnp.bfloat16)
    member_field = jnp.einsum(
        "bij,kj->bik", lat_smoothed, loc_lon, preferred_element_type=jnp.float32
    )
    partial_value = jnp.sum(ens_perts.astype(jnp.float32) * member_field, axis=0)
    pieces = partial_value.reshape(tiles, -1, partial_value.shape[1])
    received = lax.all_to_all(pieces, "tile", split_axis=0, concat_axis=0, tiled=True)
    ens_incr = jnp.einsum("dl,dij->lij", level_onehot, received, precision=lax.Precision.HIGHEST)
    state = static_scale * static_control + ens_incr
    weighted = []
    for section in range(STEPS):
        state = forward_step(state, coefs)
        weighted.append(obs_weight[section] * (state - innovation[section]))
    adjoint = weighted[STEPS - 1]
    for section in range(STEPS - 2, -1, -1):
        adjoint = adjoint_step(adjoint, coefs) + weighted[section]
    gradient = adjoint_step(adjoint, coefs)
    static_final = static_control - STEP_SIZE * (static_control + static_scale * gradient)
    outgoing = jnp.take(gradient, level_map, axis=0)
    incoming = lax.all_to_all(outgoing, "tile", split_axis=0, concat_axis=0, tiled=True)
    grad_field = incoming.reshape(-1, incoming.shape[2])
    weighted_grad = (ens_perts.astype(jnp.float32) * grad_field[None]).astype(jnp.bfloat16)
    adjoint_lat = jnp.einsum(
        "ji,bjk->bik", loc_lat, weighted_grad, preferred_element_type=jnp.float32
    ).astype(jnp.bfloat16)
    member_grad = jnp.einsum("bij,jk->bik", adjoint_lat, loc_lon, preferred_element_type=jnp.float32)
    return ens_control - STEP_SIZE * (ens_control + member_grad), static_final


def local(*args):
    levels, rows, nlon = args[5].shape
    whole = rows % SUB == 0 and nlon % LANES == 0 and levels % GROUP == 0
    return (whole_local if whole else any_local)(*args)


def solution(mesh):
    in_specs = (
        P(),
        P(),
        P(),
        P(("groups", "tile"), None, None),
        P(("groups", "tile"), None, None),
        P("groups", "tile", None),
        P("groups", "tile", None),
        P(None, "groups", "tile", None),
        P(None, "groups", "tile", None),
        P(None, "groups", "tile", None),
    )
    out_specs = (P(("groups", "tile"), None, None), P("groups", "tile", None))
    return jax.shard_map(local, mesh=mesh, in_specs=in_specs, out_specs=out_specs, check_vma=False)
```

```python
import jax
import jax.numpy as jnp
from jax import lax
from jax.experimental import pallas as pl
from jax.experimental.pallas import tpu as pltpu
from jax.sharding import PartitionSpec as P

STEPS = 3
LANES = 128
SUB = 8
STEP_SIZE = 0.15
GROUP = 4

SPILL = 2
HALO = 2 * STEPS - SPILL


def packed_fields():
    fields = [("static", 0, HALO)]
    fields += [("coefs", k, HALO - 1) for k in range(4)]
    for section in range(SPILL, STEPS):
        fields += [(name, section, section + 1 - SPILL) for name in ("obs_weight", "innovation")]
    return fields


LEVEL_ROWS = sum(rows for _, _, rows in packed_fields())
PACKED = GROUP * LEVEL_ROWS


def vmem(count):
    return [pl.BlockSpec(memory_space=pltpu.VMEM)] * count


def params(mebibytes):
    return pltpu.CompilerParams(vmem_limit_bytes=mebibytes << 20)


def order(tiles):
    return [(2 * tiles // 3 + 1 - position) % tiles for position in range(tiles)]


def sublane(shape):
    return lax.broadcasted_iota(jnp.int32, shape, 0)


def member_sum_kernel(tiles, lat_ref, lon_ref, perts_ref, control_ref, out_ref):
    blocks, nlat, nlon = control_ref.shape
    rows = nlat // tiles
    halves = nlon // LANES
    total = None
    for b in range(blocks):
        smoothed = jnp.dot(
            lat_ref[...], control_ref[b].astype(jnp.bfloat16), preferred_element_type=jnp.float32
        ).astype(jnp.bfloat16)
        field = lax.dot_general(
            smoothed, lon_ref[...], (((1,), (1,)), ((), ())), preferred_element_type=jnp.float32
        )
        term = perts_ref[b].astype(jnp.float32) * field
        total = term if total is None else total + term
    first = sublane((SUB, LANES)) < HALO
    edge = jnp.zeros((SUB, LANES), jnp.float32)
    for e, tile in enumerate(order(tiles)):
        start = tile * rows
        end = start + rows
        for h in range(halves):
            lanes = slice(h * LANES, (h + 1) * LANES)
            above = total[end : end + SUB, lanes] if end < nlat else edge
            below = total[start - SUB : start, lanes] if start > 0 else edge
            out_ref[e, h * rows : (h + 1) * rows, :] = total[start:end, lanes]
            at = halves * rows + h * SUB
            out_ref[e, at : at + SUB, :] = jnp.where(first, above, below)


def pack_kernel(control_ref, scale_ref, coefs_ref, weight_ref, innov_ref, up_ref, down_ref):
    refs = {"coefs": coefs_ref, "obs_weight": weight_ref, "innovation": innov_ref}
    levels, rows, _ = control_ref.shape
    for l in range(levels):
        at = l % GROUP * LEVEL_ROWS
        for name, k, count in packed_fields():
            last, first = slice(rows - count, rows), slice(0, count)
            if name == "static":
                high = scale_ref[l, last, :] * control_ref[l, last, :]
                low = scale_ref[l, first, :] * control_ref[l, first, :]
            else:
                high, low = refs[name][k, l, last, :], refs[name][k, l, first, :]
            up_ref[l // GROUP, at : at + count, :] = high
            down_ref[l // GROUP, at : at + count, :] = low
            at += count


def window_kernel(
    level_ref,
    received_ref,
    low_ref,
    high_ref,
    control_ref,
    scale_ref,
    coefs_ref,
    weight_ref,
    innov_ref,
    send_ref,
    grad_ref,
    up_ref,
    down_ref,
    sums_ref,
):
    tiles = received_ref.shape[0]
    levels, rows, nlon = control_ref.shape
    ring = rows + SUB
    halves = nlon // LANES
    refs = {"coefs": coefs_ref, "obs_weight": weight_ref, "innovation": innov_ref}

    sums_ref[...] = jnp.zeros_like(sums_ref)
    for d, tile in enumerate(order(tiles)):
        sums_ref[level_ref[tile]] += received_ref[d]

    above = sublane((SUB, nlon)) < HALO

    def low_rows(g, at, count):
        start = max(at + count - SUB, 0)
        block = low_ref[g, start : start + SUB, :]
        shift = SUB - (at + count - start)
        return pltpu.roll(block, shift, 0) if shift else block

    def high_rows(g, at):
        start = min(at, PACKED - SUB)
        block = high_ref[g, start : start + SUB, :]
        return pltpu.roll(block, SUB - (at - start), 0) if at > start else block

    def level(g, i):
        l = g * GROUP + i
        fields = {}
        at = i * LEVEL_ROWS
        for name, k, count in packed_fields():
            inner = scale_ref[l] * control_ref[l] if name == "static" else refs[name][k, l]
            edge = jnp.where(above, high_rows(g, at), low_rows(g, at, count))
            fields[name, k] = jnp.concatenate([inner, edge], axis=0)
            at += count
        c0, c1, c2, c3 = (fields["coefs", k] for k in range(4))
        rest = 1.0 - (c0 + c1 + c2 + c3)

        sums = []
        for h in range(halves):
            edge = halves * rows + h * SUB
            sums.append(
                jnp.concatenate(
                    [sums_ref[l, h * rows : (h + 1) * rows, :], sums_ref[l, edge : edge + SUB, :]],
                    axis=0,
                )
            )
        state = fields["static", 0] + jnp.concatenate(sums, axis=1)
        weighted = []
        for section in range(STEPS):
            state = (
                rest * state
                + c0 * pltpu.roll(state, ring - 1, 0)
                + c1 * pltpu.roll(state, 1, 0)
                + c2 * pltpu.roll(state, nlon - 1, 1)
                + c3 * pltpu.roll(state, 1, 1)
            )
            if section < SPILL:
                weighted.append(weight_ref[section, l] * (state[:rows] - innov_ref[section, l]))
            else:
                weighted.append(
                    fields["obs_weight", section] * (state - fields["innovation", section])
                )
        adjoint = weighted[STEPS - 1]
        for left in range(STEPS - 1, -1, -1):
            if left + 1 == SPILL:
                adjoint = jnp.concatenate(
                    [adjoint[:rows], jnp.zeros((SUB, nlon), jnp.float32)], axis=0
                )
            adjoint = (
                rest * adjoint
                + pltpu.roll(c0 * adjoint, 1, 0)
                + pltpu.roll(c1 * adjoint, ring - 1, 0)
                + pltpu.roll(c2 * adjoint, 1, 1)
                + pltpu.roll(c3 * adjoint, nlon - 1, 1)
            )
            if left > SPILL:
                adjoint = adjoint + weighted[left - 1]
            elif left > 0:
                adjoint = jnp.concatenate(
                    [adjoint[:rows] + weighted[left - 1], adjoint[rows:]], axis=0
                )
        grad_ref[l] = adjoint
        up_ref[g, i * SPILL : (i + 1) * SPILL, :] = adjoint[rows : rows + SPILL]
        down_ref[g, i * SPILL : (i + 1) * SPILL, :] = adjoint[ring - SPILL :]

    def group(g, carry):
        for i in range(GROUP):
            level(g, i)
        return carry

    lax.fori_loop(0, levels // GROUP, group, 0)
    row = sublane((SUB, LANES))
    for e, tile in enumerate(order(tiles)):
        at = level_ref[tile]
        for h in range(0, halves, 2):
            spilled = grad_ref[at, rows:ring, h * LANES : (h + 1) * LANES]
            if h + 1 < halves:
                block = grad_ref[at, rows:ring, (h + 1) * LANES : (h + 2) * LANES]
                middle = jnp.where(
                    row < 2 * SPILL, pltpu.roll(block, SPILL, 0), pltpu.roll(block, SUB - SPILL, 0)
                )
                outer = (row < SPILL) | (row >= SUB - SPILL)
                spilled = jnp.where(outer, spilled, middle)
            start = halves * rows + h // 2 * SUB
            send_ref[e, start : start + SUB, :] = spilled
        for h in range(halves):
            lanes = slice(h * LANES, (h + 1) * LANES)
            send_ref[e, h * rows : (h + 1) * rows, :] = grad_ref[at, 0:rows, lanes]


def member_update_kernel(
    lat_ref,
    lon_ref,
    perts_ref,
    incoming_ref,
    control_ref,
    low_ref,
    high_ref,
    tile_grad_ref,
    static_ref,
    scale_ref,
    out_ref,
    static_out_ref,
    field_ref,
):
    tiles = incoming_ref.shape[0]
    blocks, nlat, nlon = control_ref.shape
    rows = nlat // tiles
    halves = nlon // LANES
    half_row = sublane((SUB, LANES))
    position = {tile: p for p, tile in enumerate(order(tiles))}
    for h in range(halves):
        lanes = slice(h * LANES, (h + 1) * LANES)
        start = halves * rows + h // 2 * SUB
        inset = h % 2 * SPILL

        def spill(s, above):
            block = incoming_ref[position[s], start : start + SUB, :]
            if inset:
                block = pltpu.roll(block, SUB - inset if above else inset, 0)
            keep = half_row < SPILL if above else half_row >= SUB - SPILL
            return jnp.where(keep, block, 0.0)

        for s in range(tiles):
            piece = incoming_ref[position[s], h * rows : (h + 1) * rows, :]
            parts = [piece[t * SUB : (t + 1) * SUB] for t in range(rows // SUB)]
            if s > 0:
                parts[0] = parts[0] + spill(s - 1, True)
            if s < tiles - 1:
                parts[-1] = parts[-1] + spill(s + 1, False)
            field_ref[s * rows : (s + 1) * rows, lanes] = jnp.concatenate(parts, axis=0)
    for b in range(blocks):
        weighted = (perts_ref[b].astype(jnp.float32) * field_ref[...]).astype(jnp.bfloat16)
        adjoint_lat = lax.dot_general(
            lat_ref[...], weighted, (((0,), (0,)), ((), ())), preferred_element_type=jnp.float32
        ).astype(jnp.bfloat16)
        member_grad = jnp.dot(adjoint_lat, lon_ref[...], preferred_element_type=jnp.float32)
        control = control_ref[b]
        out_ref[b] = control - STEP_SIZE * (control + member_grad)

    row = sublane((SUB, nlon))
    for l in range(static_ref.shape[0]):
        at = l % GROUP * SPILL
        block = low_ref[l // GROUP, 0:SUB, :]
        above = jnp.where(row < SPILL, pltpu.roll(block, SUB - at, 0) if at else block, 0.0)
        block = high_ref[l // GROUP, 0:SUB, :]
        shift = (SUB - SPILL - at) % SUB
        below = jnp.where(
            row >= SUB - SPILL, pltpu.roll(block, shift, 0) if shift else block, 0.0
        )
        parts = [tile_grad_ref[l, t * SUB : (t + 1) * SUB, :] for t in range(rows // SUB)]
        parts[0] = parts[0] + above
        parts[-1] = parts[-1] + below
        gradient = jnp.concatenate(parts, axis=0)
        static = static_ref[l]
        static_out_ref[l] = static - STEP_SIZE * (static + scale_ref[l] * gradient)


def whole_local(
    level_map, loc_lat, loc_lon, ens_perts, ens_control,
    static_control, static_scale, coefs, obs_weight, innovation,
):
    tiles = lax.axis_size("tile")
    levels, rows, nlon = static_control.shape
    halves = nlon // LANES
    forward = [(i, i + 1) for i in range(tiles - 1)]
    backward = [(target, source) for source, target in forward]

    def swapped(pieces):
        return lax.all_to_all(
            pieces, "tile", split_axis=0, concat_axis=0, tiled=True,
            axis_index_groups=[order(tiles)],
        )

    def array(*shape):
        return jax.ShapeDtypeStruct(shape, jnp.float32)

    first_shape = (tiles, halves * (rows + SUB), LANES)
    pieces = pl.pallas_call(
        lambda *refs: member_sum_kernel(tiles, *refs),
        out_shape=array(*first_shape),
        in_specs=vmem(4),
        out_specs=vmem(1)[0],
        name="member_sum",
    )(loc_lat, loc_lon, ens_perts, ens_control)
    received = swapped(pieces)

    packed = array(levels // GROUP, PACKED, nlon)
    up, down = pl.pallas_call(
        pack_kernel,
        out_shape=(packed, packed),
        in_specs=vmem(5),
        out_specs=tuple(vmem(2)),
        compiler_params=params(8),
        name="pack",
    )(static_control, static_scale, coefs, obs_weight, innovation)
    low = lax.ppermute(up, "tile", forward)
    high = lax.ppermute(down, "tile", backward)

    spilled = array(levels // GROUP, GROUP * SPILL, nlon)
    send, tile_grad, up, down = pl.pallas_call(
        window_kernel,
        out_shape=(
            array(tiles, halves * rows + -(-halves // 2) * SUB, LANES),
            array(levels, rows + SUB, nlon),
            spilled,
            spilled,
        ),
        in_specs=[pl.BlockSpec(memory_space=pltpu.SMEM)] + vmem(8),
        out_specs=tuple(vmem(4)),
        scratch_shapes=[pltpu.VMEM((levels,) + first_shape[1:], jnp.float32)],
        compiler_params=params(8),
        name="window",
    )(level_map, received, low, high, static_control, static_scale, coefs, obs_weight, innovation)
    incoming = swapped(send)
    low = lax.ppermute(up, "tile", forward)
    high = lax.ppermute(down, "tile", backward)

    return pl.pallas_call(
        member_update_kernel,
        out_shape=(array(*ens_control.shape), array(*static_control.shape)),
        in_specs=vmem(10),
        out_specs=tuple(vmem(2)),
        scratch_shapes=[pltpu.VMEM(ens_control.shape[1:], jnp.float32)],
        compiler_params=params(8),
        name="member_update",
    )(
        loc_lat, loc_lon, ens_perts, incoming, ens_control,
        low, high, tile_grad, static_control, static_scale,
    )


def exchanged(block, axis):
    count = lax.axis_size("tile")
    forward = [(i, i + 1) for i in range(count - 1)]
    backward = [(target, source) for source, target in forward]
    last = block.shape[axis] - 1
    low = lax.ppermute(lax.slice_in_dim(block, last, last + 1, axis=axis), "tile", forward)
    high = lax.ppermute(lax.slice_in_dim(block, 0, 1, axis=axis), "tile", backward)
    return jnp.concatenate([low, block, high], axis=axis)


def forward_step(state, coeffs):
    padded = exchanged(state, 1)
    return (
        state
        + coeffs[0] * (padded[:, 2:] - state)
        + coeffs[1] * (padded[:, :-2] - state)
        + coeffs[2] * (jnp.roll(state, -1, 2) - state)
        + coeffs[3] * (jnp.roll(state, 1, 2) - state)
    )


def adjoint_step(adjoint, coeffs):
    coef_sum = coeffs[0] + coeffs[1] + coeffs[2] + coeffs[3]
    padded = exchanged(jnp.stack([coeffs[0] * adjoint, coeffs[1] * adjoint]), 2)
    return (
        (1.0 - coef_sum) * adjoint
        + padded[0][:, :-2]
        + padded[1][:, 2:]
        + jnp.roll(coeffs[2] * adjoint, 1, 2)
        + jnp.roll(coeffs[3] * adjoint, -1, 2)
    )


def any_local(
    level_map, loc_lat, loc_lon, ens_perts, ens_control,
    static_control, static_scale, coefs, obs_weight, innovation,
):
    tiles = lax.axis_size("tile")
    level_ids = jnp.arange(static_control.shape[0], dtype=jnp.int32)
    level_onehot = (level_map[:, None] == level_ids[None, :]).astype(jnp.float32)
    lat_smoothed = jnp.einsum(
        "ij,bjk->bik", loc_lat, ens_control.astype(jnp.bfloat16),
        preferred_element_type=jnp.float32,
    ).astype(jnp.bfloat16)
    member_field = jnp.einsum(
        "bij,kj->bik", lat_smoothed, loc_lon, preferred_element_type=jnp.float32
    )
    partial_value = jnp.sum(ens_perts.astype(jnp.float32) * member_field, axis=0)
    pieces = partial_value.reshape(tiles, -1, partial_value.shape[1])
    received = lax.all_to_all(pieces, "tile", split_axis=0, concat_axis=0, tiled=True)
    ens_incr = jnp.einsum("dl,dij->lij", level_onehot, received, precision=lax.Precision.HIGHEST)
    state = static_scale * static_control + ens_incr
    weighted = []
    for section in range(STEPS):
        state = forward_step(state, coefs)
        weighted.append(obs_weight[section] * (state - innovation[section]))
    adjoint = weighted[STEPS - 1]
    for section in range(STEPS - 2, -1, -1):
        adjoint = adjoint_step(adjoint, coefs) + weighted[section]
    gradient = adjoint_step(adjoint, coefs)
    static_final = static_control - STEP_SIZE * (static_control + static_scale * gradient)
    outgoing = jnp.take(gradient, level_map, axis=0)
    incoming = lax.all_to_all(outgoing, "tile", split_axis=0, concat_axis=0, tiled=True)
    grad_field = incoming.reshape(-1, incoming.shape[2])
    weighted_grad = (ens_perts.astype(jnp.float32) * grad_field[None]).astype(jnp.bfloat16)
    adjoint_lat = jnp.einsum(
        "ji,bjk->bik", loc_lat, weighted_grad, preferred_element_type=jnp.float32
    ).astype(jnp.bfloat16)
    member_grad = jnp.einsum("bij,jk->bik", adjoint_lat, loc_lon, preferred_element_type=jnp.float32)
    return ens_control - STEP_SIZE * (ens_control + member_grad), static_final


def local(*args):
    levels, rows, nlon = args[5].shape
    whole = rows % SUB == 0 and nlon % LANES == 0 and levels % GROUP == 0
    return (whole_local if whole else any_local)(*args)


def solution(mesh):
    in_specs = (
        P(),
        P(),
        P(),
        P(("groups", "tile"), None, None),
        P(("groups", "tile"), None, None),
        P("groups", "tile", None),
        P("groups", "tile", None),
        P(None, "groups", "tile", None),
        P(None, "groups", "tile", None),
        P(None, "groups", "tile", None),
    )
    out_specs = (P(("groups", "tile"), None, None), P("groups", "tile", None))
    return jax.shard_map(local, mesh=mesh, in_specs=in_specs, out_specs=out_specs, check_vma=False)
```

```python
import jax
import jax.numpy as jnp
from jax import lax
from jax.experimental import pallas as pl
from jax.experimental.pallas import tpu as pltpu
from jax.sharding import PartitionSpec as P

STEPS = 3
LANES = 128
SUB = 8
STEP_SIZE = 0.15
GROUP = 4

SPILL = 2
HALO = 2 * STEPS - SPILL


def packed_fields():
    fields = [("static", 0, HALO)]
    fields += [("coefs", k, HALO - 1) for k in range(4)]
    for section in range(SPILL, STEPS):
        fields += [(name, section, section + 1 - SPILL) for name in ("obs_weight", "innovation")]
    return fields


LEVEL_ROWS = sum(rows for _, _, rows in packed_fields())
PACKED = GROUP * LEVEL_ROWS


def vmem(count):
    return [pl.BlockSpec(memory_space=pltpu.VMEM)] * count


def params(mebibytes):
    return pltpu.CompilerParams(vmem_limit_bytes=mebibytes << 20)


def order(tiles):
    return [(2 * tiles // 3 + 1 - position) % tiles for position in range(tiles)]


def sublane(shape):
    return lax.broadcasted_iota(jnp.int32, shape, 0)


def member_sum_kernel(tiles, lat_ref, lon_ref, perts_ref, control_ref, out_ref):
    blocks, nlat, nlon = control_ref.shape
    rows = nlat // tiles
    halves = nlon // LANES
    total = None
    for b in range(blocks):
        smoothed = jnp.dot(
            lat_ref[...], control_ref[b].astype(jnp.bfloat16), preferred_element_type=jnp.float32
        ).astype(jnp.bfloat16)
        field = lax.dot_general(
            smoothed, lon_ref[...], (((1,), (1,)), ((), ())), preferred_element_type=jnp.float32
        )
        term = perts_ref[b].astype(jnp.float32) * field
        total = term if total is None else total + term
    first = sublane((SUB, LANES)) < HALO
    edge = jnp.zeros((SUB, LANES), jnp.float32)
    for e, tile in enumerate(order(tiles)):
        start = tile * rows
        end = start + rows
        for h in range(halves):
            lanes = slice(h * LANES, (h + 1) * LANES)
            above = total[end : end + SUB, lanes] if end < nlat else edge
            below = total[start - SUB : start, lanes] if start > 0 else edge
            out_ref[e, h * rows : (h + 1) * rows, :] = total[start:end, lanes]
            at = halves * rows + h * SUB
            out_ref[e, at : at + SUB, :] = jnp.where(first, above, below)


def pack_kernel(control_ref, scale_ref, coefs_ref, weight_ref, innov_ref, inner_ref, outer_ref):
    even = lax.axis_index("tile") % 2 == 0

    @pl.when(even)
    def _():
        pack(control_ref, scale_ref, coefs_ref, weight_ref, innov_ref, inner_ref, outer_ref)

    @pl.when(jnp.logical_not(even))
    def _():
        pack(control_ref, scale_ref, coefs_ref, weight_ref, innov_ref, outer_ref, inner_ref)


def pack(control_ref, scale_ref, coefs_ref, weight_ref, innov_ref, up_ref, down_ref):
    refs = {"coefs": coefs_ref, "obs_weight": weight_ref, "innovation": innov_ref}
    levels, rows, _ = control_ref.shape
    for l in range(levels):
        at = l % GROUP * LEVEL_ROWS
        for name, k, count in packed_fields():
            last, first = slice(rows - count, rows), slice(0, count)
            if name == "static":
                high = scale_ref[l, last, :] * control_ref[l, last, :]
                low = scale_ref[l, first, :] * control_ref[l, first, :]
            else:
                high, low = refs[name][k, l, last, :], refs[name][k, l, first, :]
            up_ref[l // GROUP, at : at + count, :] = high
            down_ref[l // GROUP, at : at + count, :] = low
            at += count


def window_kernel(
    level_ref,
    received_ref,
    inner_ref,
    outer_ref,
    control_ref,
    scale_ref,
    coefs_ref,
    weight_ref,
    innov_ref,
    send_ref,
    grad_ref,
    inner_out_ref,
    outer_out_ref,
    sums_ref,
    low_ref,
    high_ref,
):
    tiles = received_ref.shape[0]
    levels, rows, nlon = control_ref.shape
    ring = rows + SUB
    halves = nlon // LANES
    refs = {"coefs": coefs_ref, "obs_weight": weight_ref, "innovation": innov_ref}
    even = lax.axis_index("tile") % 2 == 0

    @pl.when(even)
    def _():
        low_ref[...] = outer_ref[...]
        high_ref[...] = inner_ref[...]

    @pl.when(jnp.logical_not(even))
    def _():
        low_ref[...] = inner_ref[...]
        high_ref[...] = outer_ref[...]

    sums_ref[...] = jnp.zeros_like(sums_ref)
    for d, tile in enumerate(order(tiles)):
        sums_ref[level_ref[tile]] += received_ref[d]

    above = sublane((SUB, nlon)) < HALO

    def low_rows(g, at, count):
        start = max(at + count - SUB, 0)
        block = low_ref[g, start : start + SUB, :]
        shift = SUB - (at + count - start)
        return pltpu.roll(block, shift, 0) if shift else block

    def high_rows(g, at):
        start = min(at, PACKED - SUB)
        block = high_ref[g, start : start + SUB, :]
        return pltpu.roll(block, SUB - (at - start), 0) if at > start else block

    def level(g, i):
        l = g * GROUP + i
        fields = {}
        at = i * LEVEL_ROWS
        for name, k, count in packed_fields():
            inner = scale_ref[l] * control_ref[l] if name == "static" else refs[name][k, l]
            edge = jnp.where(above, high_rows(g, at), low_rows(g, at, count))
            fields[name, k] = jnp.concatenate([inner, edge], axis=0)
            at += count
        c0, c1, c2, c3 = (fields["coefs", k] for k in range(4))
        rest = 1.0 - (c0 + c1 + c2 + c3)

        sums = []
        for h in range(halves):
            edge = halves * rows + h * SUB
            sums.append(
                jnp.concatenate(
                    [sums_ref[l, h * rows : (h + 1) * rows, :], sums_ref[l, edge : edge + SUB, :]],
                    axis=0,
                )
            )
        state = fields["static", 0] + jnp.concatenate(sums, axis=1)
        weighted = []
        for section in range(STEPS):
            state = (
                rest * state
                + c0 * pltpu.roll(state, ring - 1, 0)
                + c1 * pltpu.roll(state, 1, 0)
                + c2 * pltpu.roll(state, nlon - 1, 1)
                + c3 * pltpu.roll(state, 1, 1)
            )
            if section < SPILL:
                weighted.append(weight_ref[section, l] * (state[:rows] - innov_ref[section, l]))
            else:
                weighted.append(
                    fields["obs_weight", section] * (state - fields["innovation", section])
                )
        adjoint = weighted[STEPS - 1]
        for left in range(STEPS - 1, -1, -1):
            if left + 1 == SPILL:
                adjoint = jnp.concatenate(
                    [adjoint[:rows], jnp.zeros((SUB, nlon), jnp.float32)], axis=0
                )
            adjoint = (
                rest * adjoint
                + pltpu.roll(c0 * adjoint, 1, 0)
                + pltpu.roll(c1 * adjoint, ring - 1, 0)
                + pltpu.roll(c2 * adjoint, 1, 1)
                + pltpu.roll(c3 * adjoint, nlon - 1, 1)
            )
            if left > SPILL:
                adjoint = adjoint + weighted[left - 1]
            elif left > 0:
                adjoint = jnp.concatenate(
                    [adjoint[:rows] + weighted[left - 1], adjoint[rows:]], axis=0
                )
        grad_ref[l] = adjoint
        above_rows, below_rows = adjoint[rows : rows + SPILL], adjoint[ring - SPILL :]
        spot = slice(i * SPILL, (i + 1) * SPILL)
        inner_out_ref[g, spot, :] = jnp.where(even, above_rows, below_rows)
        outer_out_ref[g, spot, :] = jnp.where(even, below_rows, above_rows)

    for l in range(levels):
        level(l // GROUP, l % GROUP)
    row = sublane((SUB, LANES))
    for e, tile in enumerate(order(tiles)):
        at = level_ref[tile]
        for h in range(0, halves, 2):
            spilled = grad_ref[at, rows:ring, h * LANES : (h + 1) * LANES]
            if h + 1 < halves:
                block = grad_ref[at, rows:ring, (h + 1) * LANES : (h + 2) * LANES]
                middle = jnp.where(
                    row < 2 * SPILL, pltpu.roll(block, SPILL, 0), pltpu.roll(block, SUB - SPILL, 0)
                )
                outer = (row < SPILL) | (row >= SUB - SPILL)
                spilled = jnp.where(outer, spilled, middle)
            start = halves * rows + h // 2 * SUB
            send_ref[e, start : start + SUB, :] = spilled
        for h in range(halves):
            lanes = slice(h * LANES, (h + 1) * LANES)
            send_ref[e, h * rows : (h + 1) * rows, :] = grad_ref[at, 0:rows, lanes]


def member_update_kernel(
    lat_ref,
    lon_ref,
    perts_ref,
    incoming_ref,
    control_ref,
    inner_ref,
    outer_ref,
    tile_grad_ref,
    static_ref,
    scale_ref,
    out_ref,
    static_out_ref,
    field_ref,
):
    tiles = incoming_ref.shape[0]
    blocks, nlat, nlon = control_ref.shape
    rows = nlat // tiles
    halves = nlon // LANES
    half_row = sublane((SUB, LANES))
    position = {tile: p for p, tile in enumerate(order(tiles))}
    for h in range(halves):
        lanes = slice(h * LANES, (h + 1) * LANES)
        start = halves * rows + h // 2 * SUB
        inset = h % 2 * SPILL

        def spill(s, above):
            block = incoming_ref[position[s], start : start + SUB, :]
            if inset:
                block = pltpu.roll(block, SUB - inset if above else inset, 0)
            keep = half_row < SPILL if above else half_row >= SUB - SPILL
            return jnp.where(keep, block, 0.0)

        for s in range(tiles):
            piece = incoming_ref[position[s], h * rows : (h + 1) * rows, :]
            parts = [piece[t * SUB : (t + 1) * SUB] for t in range(rows // SUB)]
            if s > 0:
                parts[0] = parts[0] + spill(s - 1, True)
            if s < tiles - 1:
                parts[-1] = parts[-1] + spill(s + 1, False)
            field_ref[s * rows : (s + 1) * rows, lanes] = jnp.concatenate(parts, axis=0)
    for b in range(blocks):
        weighted = (perts_ref[b].astype(jnp.float32) * field_ref[...]).astype(jnp.bfloat16)
        adjoint_lat = lax.dot_general(
            lat_ref[...], weighted, (((0,), (0,)), ((), ())), preferred_element_type=jnp.float32
        ).astype(jnp.bfloat16)
        member_grad = jnp.dot(adjoint_lat, lon_ref[...], preferred_element_type=jnp.float32)
        control = control_ref[b]
        out_ref[b] = control - STEP_SIZE * (control + member_grad)

    row = sublane((SUB, nlon))
    even = lax.axis_index("tile") % 2 == 0
    for l in range(static_ref.shape[0]):
        at = l % GROUP * SPILL
        inner, outer = inner_ref[l // GROUP, 0:SUB, :], outer_ref[l // GROUP, 0:SUB, :]
        block = jnp.where(even, outer, inner)
        above = jnp.where(row < SPILL, pltpu.roll(block, SUB - at, 0) if at else block, 0.0)
        block = jnp.where(even, inner, outer)
        shift = (SUB - SPILL - at) % SUB
        below = jnp.where(
            row >= SUB - SPILL, pltpu.roll(block, shift, 0) if shift else block, 0.0
        )
        parts = [tile_grad_ref[l, t * SUB : (t + 1) * SUB, :] for t in range(rows // SUB)]
        parts[0] = parts[0] + above
        parts[-1] = parts[-1] + below
        gradient = jnp.concatenate(parts, axis=0)
        static = static_ref[l]
        static_out_ref[l] = static - STEP_SIZE * (static + scale_ref[l] * gradient)


def whole_local(
    level_map, loc_lat, loc_lon, ens_perts, ens_control,
    static_control, static_scale, coefs, obs_weight, innovation,
):
    tiles = lax.axis_size("tile")
    levels, rows, nlon = static_control.shape
    halves = nlon // LANES

    def exchanged_pairs(inner, outer):
        pairs = [[(i, i + 1) for i in range(first, tiles - 1, 2)] for first in (0, 1)]
        both = [pair + [(b, a) for a, b in pair] for pair in pairs]
        return lax.ppermute(inner, "tile", both[0]), lax.ppermute(outer, "tile", both[1])

    def swapped(pieces):
        return lax.all_to_all(
            pieces, "tile", split_axis=0, concat_axis=0, tiled=True,
            axis_index_groups=[order(tiles)],
        )

    def array(*shape):
        return jax.ShapeDtypeStruct(shape, jnp.float32)

    first_shape = (tiles, halves * (rows + SUB), LANES)
    pieces = pl.pallas_call(
        lambda *refs: member_sum_kernel(tiles, *refs),
        out_shape=array(*first_shape),
        in_specs=vmem(4),
        out_specs=vmem(1)[0],
        name="member_sum",
    )(loc_lat, loc_lon, ens_perts, ens_control)
    received = swapped(pieces)

    packed = array(levels // GROUP, PACKED, nlon)
    inner, outer = pl.pallas_call(
        pack_kernel,
        out_shape=(packed, packed),
        in_specs=vmem(5),
        out_specs=tuple(vmem(2)),
        compiler_params=params(8),
        name="pack",
    )(static_control, static_scale, coefs, obs_weight, innovation)
    inner, outer = exchanged_pairs(inner, outer)

    spilled = array(levels // GROUP, GROUP * SPILL, nlon)
    send, tile_grad, inner, outer = pl.pallas_call(
        window_kernel,
        out_shape=(
            array(tiles, halves * rows + -(-halves // 2) * SUB, LANES),
            array(levels, rows + SUB, nlon),
            spilled,
            spilled,
        ),
        in_specs=[pl.BlockSpec(memory_space=pltpu.SMEM)] + vmem(8),
        out_specs=tuple(vmem(4)),
        scratch_shapes=[
            pltpu.VMEM((levels,) + first_shape[1:], jnp.float32),
            pltpu.VMEM(packed.shape, jnp.float32),
            pltpu.VMEM(packed.shape, jnp.float32),
        ],
        compiler_params=params(8),
        name="window",
    )(level_map, received, inner, outer, static_control, static_scale, coefs, obs_weight, innovation)
    incoming = swapped(send)
    inner, outer = exchanged_pairs(inner, outer)

    return pl.pallas_call(
        member_update_kernel,
        out_shape=(array(*ens_control.shape), array(*static_control.shape)),
        in_specs=vmem(10),
        out_specs=tuple(vmem(2)),
        scratch_shapes=[pltpu.VMEM(ens_control.shape[1:], jnp.float32)],
        compiler_params=params(8),
        name="member_update",
    )(
        loc_lat, loc_lon, ens_perts, incoming, ens_control,
        inner, outer, tile_grad, static_control, static_scale,
    )


def exchanged(block, axis):
    count = lax.axis_size("tile")
    forward = [(i, i + 1) for i in range(count - 1)]
    backward = [(target, source) for source, target in forward]
    last = block.shape[axis] - 1
    low = lax.ppermute(lax.slice_in_dim(block, last, last + 1, axis=axis), "tile", forward)
    high = lax.ppermute(lax.slice_in_dim(block, 0, 1, axis=axis), "tile", backward)
    return jnp.concatenate([low, block, high], axis=axis)


def forward_step(state, coeffs):
    padded = exchanged(state, 1)
    return (
        state
        + coeffs[0] * (padded[:, 2:] - state)
        + coeffs[1] * (padded[:, :-2] - state)
        + coeffs[2] * (jnp.roll(state, -1, 2) - state)
        + coeffs[3] * (jnp.roll(state, 1, 2) - state)
    )


def adjoint_step(adjoint, coeffs):
    coef_sum = coeffs[0] + coeffs[1] + coeffs[2] + coeffs[3]
    padded = exchanged(jnp.stack([coeffs[0] * adjoint, coeffs[1] * adjoint]), 2)
    return (
        (1.0 - coef_sum) * adjoint
        + padded[0][:, :-2]
        + padded[1][:, 2:]
        + jnp.roll(coeffs[2] * adjoint, 1, 2)
        + jnp.roll(coeffs[3] * adjoint, -1, 2)
    )


def any_local(
    level_map, loc_lat, loc_lon, ens_perts, ens_control,
    static_control, static_scale, coefs, obs_weight, innovation,
):
    tiles = lax.axis_size("tile")
    level_ids = jnp.arange(static_control.shape[0], dtype=jnp.int32)
    level_onehot = (level_map[:, None] == level_ids[None, :]).astype(jnp.float32)
    lat_smoothed = jnp.einsum(
        "ij,bjk->bik", loc_lat, ens_control.astype(jnp.bfloat16),
        preferred_element_type=jnp.float32,
    ).astype(jnp.bfloat16)
    member_field = jnp.einsum(
        "bij,kj->bik", lat_smoothed, loc_lon, preferred_element_type=jnp.float32
    )
    partial_value = jnp.sum(ens_perts.astype(jnp.float32) * member_field, axis=0)
    pieces = partial_value.reshape(tiles, -1, partial_value.shape[1])
    received = lax.all_to_all(pieces, "tile", split_axis=0, concat_axis=0, tiled=True)
    ens_incr = jnp.einsum("dl,dij->lij", level_onehot, received, precision=lax.Precision.HIGHEST)
    state = static_scale * static_control + ens_incr
    weighted = []
    for section in range(STEPS):
        state = forward_step(state, coefs)
        weighted.append(obs_weight[section] * (state - innovation[section]))
    adjoint = weighted[STEPS - 1]
    for section in range(STEPS - 2, -1, -1):
        adjoint = adjoint_step(adjoint, coefs) + weighted[section]
    gradient = adjoint_step(adjoint, coefs)
    static_final = static_control - STEP_SIZE * (static_control + static_scale * gradient)
    outgoing = jnp.take(gradient, level_map, axis=0)
    incoming = lax.all_to_all(outgoing, "tile", split_axis=0, concat_axis=0, tiled=True)
    grad_field = incoming.reshape(-1, incoming.shape[2])
    weighted_grad = (ens_perts.astype(jnp.float32) * grad_field[None]).astype(jnp.bfloat16)
    adjoint_lat = jnp.einsum(
        "ji,bjk->bik", loc_lat, weighted_grad, preferred_element_type=jnp.float32
    ).astype(jnp.bfloat16)
    member_grad = jnp.einsum("bij,jk->bik", adjoint_lat, loc_lon, preferred_element_type=jnp.float32)
    return ens_control - STEP_SIZE * (ens_control + member_grad), static_final


def local(*args):
    levels, rows, nlon = args[5].shape
    whole = rows % SUB == 0 and nlon % LANES == 0 and levels % GROUP == 0
    return (whole_local if whole else any_local)(*args)


def solution(mesh):
    in_specs = (
        P(),
        P(),
        P(),
        P(("groups", "tile"), None, None),
        P(("groups", "tile"), None, None),
        P("groups", "tile", None),
        P("groups", "tile", None),
        P(None, "groups", "tile", None),
        P(None, "groups", "tile", None),
        P(None, "groups", "tile", None),
    )
    out_specs = (P(("groups", "tile"), None, None), P("groups", "tile", None))
    return jax.shard_map(local, mesh=mesh, in_specs=in_specs, out_specs=out_specs, check_vma=False)
```

```python
import jax
import jax.numpy as jnp
from jax import lax
from jax.experimental import pallas as pl
from jax.experimental.pallas import tpu as pltpu
from jax.sharding import PartitionSpec as P

STEPS = 3
LANES = 128
SUB = 8
STEP_SIZE = 0.15
GROUP = 4

SPILL = 2
HALO = 2 * STEPS - SPILL


def packed_fields():
    fields = [("static", 0, HALO)]
    fields += [("coefs", k, HALO - 1) for k in range(4)]
    for section in range(SPILL, STEPS):
        fields += [(name, section, section + 1 - SPILL) for name in ("obs_weight", "innovation")]
    return fields


LEVEL_ROWS = sum(rows for _, _, rows in packed_fields())
PACKED = GROUP * LEVEL_ROWS


def vmem(count):
    return [pl.BlockSpec(memory_space=pltpu.VMEM)] * count


def params(mebibytes):
    return pltpu.CompilerParams(vmem_limit_bytes=mebibytes << 20)


def order(tiles):
    quarters = [list(range(q * tiles // 4, (q + 1) * tiles // 4))[::-1] for q in (2, 0, 1, 3)]
    return sum(quarters, [])


def sublane(shape):
    return lax.broadcasted_iota(jnp.int32, shape, 0)


def member_sum_kernel(tiles, lat_ref, lon_ref, perts_ref, control_ref, out_ref):
    blocks, nlat, nlon = control_ref.shape
    rows = nlat // tiles
    halves = nlon // LANES
    total = None
    for b in range(blocks):
        smoothed = jnp.dot(
            lat_ref[...], control_ref[b].astype(jnp.bfloat16), preferred_element_type=jnp.float32
        ).astype(jnp.bfloat16)
        field = lax.dot_general(
            smoothed, lon_ref[...], (((1,), (1,)), ((), ())), preferred_element_type=jnp.float32
        )
        term = perts_ref[b].astype(jnp.float32) * field
        total = term if total is None else total + term
    first = sublane((SUB, LANES)) < HALO
    edge = jnp.zeros((SUB, LANES), jnp.float32)
    for e, tile in enumerate(order(tiles)):
        start = tile * rows
        end = start + rows
        for h in range(halves):
            lanes = slice(h * LANES, (h + 1) * LANES)
            above = total[end : end + SUB, lanes] if end < nlat else edge
            below = total[start - SUB : start, lanes] if start > 0 else edge
            out_ref[e, h * rows : (h + 1) * rows, :] = total[start:end, lanes]
            at = halves * rows + h * SUB
            out_ref[e, at : at + SUB, :] = jnp.where(first, above, below)


def pack_kernel(control_ref, scale_ref, coefs_ref, weight_ref, innov_ref, inner_ref, outer_ref):
    even = lax.axis_index("tile") % 2 == 0

    @pl.when(even)
    def _():
        pack(control_ref, scale_ref, coefs_ref, weight_ref, innov_ref, inner_ref, outer_ref)

    @pl.when(jnp.logical_not(even))
    def _():
        pack(control_ref, scale_ref, coefs_ref, weight_ref, innov_ref, outer_ref, inner_ref)


def pack(control_ref, scale_ref, coefs_ref, weight_ref, innov_ref, up_ref, down_ref):
    refs = {"coefs": coefs_ref, "obs_weight": weight_ref, "innovation": innov_ref}
    levels, rows, _ = control_ref.shape
    for l in range(levels):
        at = l % GROUP * LEVEL_ROWS
        for name, k, count in packed_fields():
            last, first = slice(rows - count, rows), slice(0, count)
            if name == "static":
                high = scale_ref[l, last, :] * control_ref[l, last, :]
                low = scale_ref[l, first, :] * control_ref[l, first, :]
            else:
                high, low = refs[name][k, l, last, :], refs[name][k, l, first, :]
            up_ref[l // GROUP, at : at + count, :] = high
            down_ref[l // GROUP, at : at + count, :] = low
            at += count


def window_kernel(
    level_ref,
    received_ref,
    inner_ref,
    outer_ref,
    control_ref,
    scale_ref,
    coefs_ref,
    weight_ref,
    innov_ref,
    send_ref,
    grad_ref,
    inner_out_ref,
    outer_out_ref,
    sums_ref,
    low_ref,
    high_ref,
):
    tiles = received_ref.shape[0]
    levels, rows, nlon = control_ref.shape
    ring = rows + SUB
    halves = nlon // LANES
    refs = {"coefs": coefs_ref, "obs_weight": weight_ref, "innovation": innov_ref}
    even = lax.axis_index("tile") % 2 == 0

    @pl.when(even)
    def _():
        low_ref[...] = outer_ref[...]
        high_ref[...] = inner_ref[...]

    @pl.when(jnp.logical_not(even))
    def _():
        low_ref[...] = inner_ref[...]
        high_ref[...] = outer_ref[...]

    sums_ref[...] = jnp.zeros_like(sums_ref)
    for d, tile in enumerate(order(tiles)):
        sums_ref[level_ref[tile]] += received_ref[d]

    above = sublane((SUB, nlon)) < HALO

    def low_rows(g, at, count):
        start = max(at + count - SUB, 0)
        block = low_ref[g, start : start + SUB, :]
        shift = SUB - (at + count - start)
        return pltpu.roll(block, shift, 0) if shift else block

    def high_rows(g, at):
        start = min(at, PACKED - SUB)
        block = high_ref[g, start : start + SUB, :]
        return pltpu.roll(block, SUB - (at - start), 0) if at > start else block

    def level(g, i):
        l = g * GROUP + i
        fields = {}
        at = i * LEVEL_ROWS
        for name, k, count in packed_fields():
            inner = scale_ref[l] * control_ref[l] if name == "static" else refs[name][k, l]
            edge = jnp.where(above, high_rows(g, at), low_rows(g, at, count))
            fields[name, k] = jnp.concatenate([inner, edge], axis=0)
            at += count
        c0, c1, c2, c3 = (fields["coefs", k] for k in range(4))
        rest = 1.0 - (c0 + c1 + c2 + c3)

        sums = []
        for h in range(halves):
            edge = halves * rows + h * SUB
            sums.append(
                jnp.concatenate(
                    [sums_ref[l, h * rows : (h + 1) * rows, :], sums_ref[l, edge : edge + SUB, :]],
                    axis=0,
                )
            )
        state = fields["static", 0] + jnp.concatenate(sums, axis=1)
        weighted = []
        for section in range(STEPS):
            state = (
                rest * state
                + c0 * pltpu.roll(state, ring - 1, 0)
                + c1 * pltpu.roll(state, 1, 0)
                + c2 * pltpu.roll(state, nlon - 1, 1)
                + c3 * pltpu.roll(state, 1, 1)
            )
            if section < SPILL:
                weighted.append(weight_ref[section, l] * (state[:rows] - innov_ref[section, l]))
            else:
                weighted.append(
                    fields["obs_weight", section] * (state - fields["innovation", section])
                )
        adjoint = weighted[STEPS - 1]
        for left in range(STEPS - 1, -1, -1):
            if left + 1 == SPILL:
                adjoint = jnp.concatenate(
                    [adjoint[:rows], jnp.zeros((SUB, nlon), jnp.float32)], axis=0
                )
            adjoint = (
                rest * adjoint
                + pltpu.roll(c0 * adjoint, 1, 0)
                + pltpu.roll(c1 * adjoint, ring - 1, 0)
                + pltpu.roll(c2 * adjoint, 1, 1)
                + pltpu.roll(c3 * adjoint, nlon - 1, 1)
            )
            if left > SPILL:
                adjoint = adjoint + weighted[left - 1]
            elif left > 0:
                adjoint = jnp.concatenate(
                    [adjoint[:rows] + weighted[left - 1], adjoint[rows:]], axis=0
                )
        grad_ref[l] = adjoint
        above_rows, below_rows = adjoint[rows : rows + SPILL], adjoint[ring - SPILL :]
        spot = slice(i * SPILL, (i + 1) * SPILL)
        inner_out_ref[g, spot, :] = jnp.where(even, above_rows, below_rows)
        outer_out_ref[g, spot, :] = jnp.where(even, below_rows, above_rows)

    for l in range(levels):
        level(l // GROUP, l % GROUP)
    row = sublane((SUB, LANES))
    for e, tile in enumerate(order(tiles)):
        at = level_ref[tile]
        for h in range(0, halves, 2):
            spilled = grad_ref[at, rows:ring, h * LANES : (h + 1) * LANES]
            if h + 1 < halves:
                block = grad_ref[at, rows:ring, (h + 1) * LANES : (h + 2) * LANES]
                middle = jnp.where(
                    row < 2 * SPILL, pltpu.roll(block, SPILL, 0), pltpu.roll(block, SUB - SPILL, 0)
                )
                outer = (row < SPILL) | (row >= SUB - SPILL)
                spilled = jnp.where(outer, spilled, middle)
            start = halves * rows + h // 2 * SUB
            send_ref[e, start : start + SUB, :] = spilled
        for h in range(halves):
            lanes = slice(h * LANES, (h + 1) * LANES)
            send_ref[e, h * rows : (h + 1) * rows, :] = grad_ref[at, 0:rows, lanes]


def member_update_kernel(
    lat_ref,
    lon_ref,
    perts_ref,
    incoming_ref,
    control_ref,
    inner_ref,
    outer_ref,
    tile_grad_ref,
    static_ref,
    scale_ref,
    out_ref,
    static_out_ref,
    field_ref,
):
    tiles = incoming_ref.shape[0]
    blocks, nlat, nlon = control_ref.shape
    rows = nlat // tiles
    halves = nlon // LANES
    half_row = sublane((SUB, LANES))
    position = {tile: p for p, tile in enumerate(order(tiles))}
    for h in range(halves):
        lanes = slice(h * LANES, (h + 1) * LANES)
        start = halves * rows + h // 2 * SUB
        inset = h % 2 * SPILL

        def spill(s, above):
            block = incoming_ref[position[s], start : start + SUB, :]
            if inset:
                block = pltpu.roll(block, SUB - inset if above else inset, 0)
            keep = half_row < SPILL if above else half_row >= SUB - SPILL
            return jnp.where(keep, block, 0.0)

        for s in range(tiles):
            piece = incoming_ref[position[s], h * rows : (h + 1) * rows, :]
            parts = [piece[t * SUB : (t + 1) * SUB] for t in range(rows // SUB)]
            if s > 0:
                parts[0] = parts[0] + spill(s - 1, True)
            if s < tiles - 1:
                parts[-1] = parts[-1] + spill(s + 1, False)
            field_ref[s * rows : (s + 1) * rows, lanes] = jnp.concatenate(parts, axis=0)
    for b in range(blocks):
        weighted = (perts_ref[b].astype(jnp.float32) * field_ref[...]).astype(jnp.bfloat16)
        adjoint_lat = lax.dot_general(
            lat_ref[...], weighted, (((0,), (0,)), ((), ())), preferred_element_type=jnp.float32
        ).astype(jnp.bfloat16)
        member_grad = jnp.dot(adjoint_lat, lon_ref[...], preferred_element_type=jnp.float32)
        control = control_ref[b]
        out_ref[b] = control - STEP_SIZE * (control + member_grad)

    row = sublane((SUB, nlon))
    even = lax.axis_index("tile") % 2 == 0
    for l in range(static_ref.shape[0]):
        at = l % GROUP * SPILL
        inner, outer = inner_ref[l // GROUP, 0:SUB, :], outer_ref[l // GROUP, 0:SUB, :]
        block = jnp.where(even, outer, inner)
        above = jnp.where(row < SPILL, pltpu.roll(block, SUB - at, 0) if at else block, 0.0)
        block = jnp.where(even, inner, outer)
        shift = (SUB - SPILL - at) % SUB
        below = jnp.where(
            row >= SUB - SPILL, pltpu.roll(block, shift, 0) if shift else block, 0.0
        )
        parts = [tile_grad_ref[l, t * SUB : (t + 1) * SUB, :] for t in range(rows // SUB)]
        parts[0] = parts[0] + above
        parts[-1] = parts[-1] + below
        gradient = jnp.concatenate(parts, axis=0)
        static = static_ref[l]
        static_out_ref[l] = static - STEP_SIZE * (static + scale_ref[l] * gradient)


def whole_local(
    level_map, loc_lat, loc_lon, ens_perts, ens_control,
    static_control, static_scale, coefs, obs_weight, innovation,
):
    tiles = lax.axis_size("tile")
    levels, rows, nlon = static_control.shape
    halves = nlon // LANES

    def exchanged_pairs(inner, outer):
        pairs = [[(i, i + 1) for i in range(first, tiles - 1, 2)] for first in (0, 1)]
        both = [pair + [(b, a) for a, b in pair] for pair in pairs]
        return lax.ppermute(inner, "tile", both[0]), lax.ppermute(outer, "tile", both[1])

    def swapped(pieces):
        return lax.all_to_all(
            pieces, "tile", split_axis=0, concat_axis=0, tiled=True,
            axis_index_groups=[order(tiles)],
        )

    def array(*shape):
        return jax.ShapeDtypeStruct(shape, jnp.float32)

    first_shape = (tiles, halves * (rows + SUB), LANES)
    pieces = pl.pallas_call(
        lambda *refs: member_sum_kernel(tiles, *refs),
        out_shape=array(*first_shape),
        in_specs=vmem(4),
        out_specs=vmem(1)[0],
        name="member_sum",
    )(loc_lat, loc_lon, ens_perts, ens_control)
    received = swapped(pieces)

    packed = array(levels // GROUP, PACKED, nlon)
    inner, outer = pl.pallas_call(
        pack_kernel,
        out_shape=(packed, packed),
        in_specs=vmem(5),
        out_specs=tuple(vmem(2)),
        compiler_params=params(8),
        name="pack",
    )(static_control, static_scale, coefs, obs_weight, innovation)
    inner, outer = exchanged_pairs(inner, outer)

    spilled = array(levels // GROUP, GROUP * SPILL, nlon)
    send, tile_grad, inner, outer = pl.pallas_call(
        window_kernel,
        out_shape=(
            array(tiles, halves * rows + -(-halves // 2) * SUB, LANES),
            array(levels, rows + SUB, nlon),
            spilled,
            spilled,
        ),
        in_specs=[pl.BlockSpec(memory_space=pltpu.SMEM)] + vmem(8),
        out_specs=tuple(vmem(4)),
        scratch_shapes=[
            pltpu.VMEM((levels,) + first_shape[1:], jnp.float32),
            pltpu.VMEM(packed.shape, jnp.float32),
            pltpu.VMEM(packed.shape, jnp.float32),
        ],
        compiler_params=params(8),
        name="window",
    )(level_map, received, inner, outer, static_control, static_scale, coefs, obs_weight, innovation)
    incoming = swapped(send)
    inner, outer = exchanged_pairs(inner, outer)

    return pl.pallas_call(
        member_update_kernel,
        out_shape=(array(*ens_control.shape), array(*static_control.shape)),
        in_specs=vmem(10),
        out_specs=tuple(vmem(2)),
        scratch_shapes=[pltpu.VMEM(ens_control.shape[1:], jnp.float32)],
        compiler_params=params(8),
        name="member_update",
    )(
        loc_lat, loc_lon, ens_perts, incoming, ens_control,
        inner, outer, tile_grad, static_control, static_scale,
    )


def exchanged(block, axis):
    count = lax.axis_size("tile")
    forward = [(i, i + 1) for i in range(count - 1)]
    backward = [(target, source) for source, target in forward]
    last = block.shape[axis] - 1
    low = lax.ppermute(lax.slice_in_dim(block, last, last + 1, axis=axis), "tile", forward)
    high = lax.ppermute(lax.slice_in_dim(block, 0, 1, axis=axis), "tile", backward)
    return jnp.concatenate([low, block, high], axis=axis)


def forward_step(state, coeffs):
    padded = exchanged(state, 1)
    return (
        state
        + coeffs[0] * (padded[:, 2:] - state)
        + coeffs[1] * (padded[:, :-2] - state)
        + coeffs[2] * (jnp.roll(state, -1, 2) - state)
        + coeffs[3] * (jnp.roll(state, 1, 2) - state)
    )


def adjoint_step(adjoint, coeffs):
    coef_sum = coeffs[0] + coeffs[1] + coeffs[2] + coeffs[3]
    padded = exchanged(jnp.stack([coeffs[0] * adjoint, coeffs[1] * adjoint]), 2)
    return (
        (1.0 - coef_sum) * adjoint
        + padded[0][:, :-2]
        + padded[1][:, 2:]
        + jnp.roll(coeffs[2] * adjoint, 1, 2)
        + jnp.roll(coeffs[3] * adjoint, -1, 2)
    )


def any_local(
    level_map, loc_lat, loc_lon, ens_perts, ens_control,
    static_control, static_scale, coefs, obs_weight, innovation,
):
    tiles = lax.axis_size("tile")
    level_ids = jnp.arange(static_control.shape[0], dtype=jnp.int32)
    level_onehot = (level_map[:, None] == level_ids[None, :]).astype(jnp.float32)
    lat_smoothed = jnp.einsum(
        "ij,bjk->bik", loc_lat, ens_control.astype(jnp.bfloat16),
        preferred_element_type=jnp.float32,
    ).astype(jnp.bfloat16)
    member_field = jnp.einsum(
        "bij,kj->bik", lat_smoothed, loc_lon, preferred_element_type=jnp.float32
    )
    partial_value = jnp.sum(ens_perts.astype(jnp.float32) * member_field, axis=0)
    pieces = partial_value.reshape(tiles, -1, partial_value.shape[1])
    received = lax.all_to_all(pieces, "tile", split_axis=0, concat_axis=0, tiled=True)
    ens_incr = jnp.einsum("dl,dij->lij", level_onehot, received, precision=lax.Precision.HIGHEST)
    state = static_scale * static_control + ens_incr
    weighted = []
    for section in range(STEPS):
        state = forward_step(state, coefs)
        weighted.append(obs_weight[section] * (state - innovation[section]))
    adjoint = weighted[STEPS - 1]
    for section in range(STEPS - 2, -1, -1):
        adjoint = adjoint_step(adjoint, coefs) + weighted[section]
    gradient = adjoint_step(adjoint, coefs)
    static_final = static_control - STEP_SIZE * (static_control + static_scale * gradient)
    outgoing = jnp.take(gradient, level_map, axis=0)
    incoming = lax.all_to_all(outgoing, "tile", split_axis=0, concat_axis=0, tiled=True)
    grad_field = incoming.reshape(-1, incoming.shape[2])
    weighted_grad = (ens_perts.astype(jnp.float32) * grad_field[None]).astype(jnp.bfloat16)
    adjoint_lat = jnp.einsum(
        "ji,bjk->bik", loc_lat, weighted_grad, preferred_element_type=jnp.float32
    ).astype(jnp.bfloat16)
    member_grad = jnp.einsum("bij,jk->bik", adjoint_lat, loc_lon, preferred_element_type=jnp.float32)
    return ens_control - STEP_SIZE * (ens_control + member_grad), static_final


def local(*args):
    levels, rows, nlon = args[5].shape
    whole = rows % SUB == 0 and nlon % LANES == 0 and levels % GROUP == 0
    return (whole_local if whole else any_local)(*args)


def solution(mesh):
    in_specs = (
        P(),
        P(),
        P(),
        P(("groups", "tile"), None, None),
        P(("groups", "tile"), None, None),
        P("groups", "tile", None),
        P("groups", "tile", None),
        P(None, "groups", "tile", None),
        P(None, "groups", "tile", None),
        P(None, "groups", "tile", None),
    )
    out_specs = (P(("groups", "tile"), None, None), P("groups", "tile", None))
    return jax.shard_map(local, mesh=mesh, in_specs=in_specs, out_specs=out_specs, check_vma=False)
```

```python
import jax
import jax.numpy as jnp
from jax import lax
from jax.experimental import pallas as pl
from jax.experimental.pallas import tpu as pltpu
from jax.sharding import PartitionSpec as P

STEPS = 3
LANES = 128
SUB = 8
STEP_SIZE = 0.15
GROUP = 4

SPILL = 2
HALO = 2 * STEPS - SPILL


def packed_fields():
    fields = [("static", 0, HALO)]
    fields += [("coefs", k, HALO - 1) for k in range(4)]
    for section in range(SPILL, STEPS):
        fields += [(name, section, section + 1 - SPILL) for name in ("obs_weight", "innovation")]
    return fields


LEVEL_ROWS = sum(rows for _, _, rows in packed_fields())
PACKED = GROUP * LEVEL_ROWS


def vmem(count):
    return [pl.BlockSpec(memory_space=pltpu.VMEM)] * count


def params(mebibytes):
    return pltpu.CompilerParams(vmem_limit_bytes=mebibytes << 20)


def order(tiles):
    quarters = [list(range(q * tiles // 4, (q + 1) * tiles // 4))[::-1] for q in (2, 0, 1, 3)]
    return sum(quarters, [])


def sublane(shape):
    return lax.broadcasted_iota(jnp.int32, shape, 0)


def member_sum_kernel(tiles, lat_ref, lon_ref, perts_ref, control_ref, out_ref):
    blocks, nlat, nlon = control_ref.shape
    rows = nlat // tiles
    halves = nlon // LANES
    total = None
    for b in range(blocks):
        smoothed = jnp.dot(
            lat_ref[...], control_ref[b].astype(jnp.bfloat16), preferred_element_type=jnp.float32
        ).astype(jnp.bfloat16)
        field = lax.dot_general(
            smoothed, lon_ref[...], (((1,), (1,)), ((), ())), preferred_element_type=jnp.float32
        )
        term = perts_ref[b].astype(jnp.float32) * field
        total = term if total is None else total + term
    first = sublane((SUB, LANES)) < HALO
    edge = jnp.zeros((SUB, LANES), jnp.float32)
    for e, tile in enumerate(order(tiles)):
        start = tile * rows
        end = start + rows
        for h in range(halves):
            lanes = slice(h * LANES, (h + 1) * LANES)
            above = total[end : end + SUB, lanes] if end < nlat else edge
            below = total[start - SUB : start, lanes] if start > 0 else edge
            out_ref[e, h * rows : (h + 1) * rows, :] = total[start:end, lanes]
            at = halves * rows + h * SUB
            out_ref[e, at : at + SUB, :] = jnp.where(first, above, below)


def pack_kernel(control_ref, scale_ref, coefs_ref, weight_ref, innov_ref, inner_ref, outer_ref):
    even = lax.axis_index("tile") % 2 == 0

    @pl.when(even)
    def _():
        pack(control_ref, scale_ref, coefs_ref, weight_ref, innov_ref, inner_ref, outer_ref)

    @pl.when(jnp.logical_not(even))
    def _():
        pack(control_ref, scale_ref, coefs_ref, weight_ref, innov_ref, outer_ref, inner_ref)


def pack(control_ref, scale_ref, coefs_ref, weight_ref, innov_ref, up_ref, down_ref):
    refs = {"coefs": coefs_ref, "obs_weight": weight_ref, "innovation": innov_ref}
    levels, rows, _ = control_ref.shape
    for l in range(levels):
        at = l % GROUP * LEVEL_ROWS
        for name, k, count in packed_fields():
            last, first = slice(rows - count, rows), slice(0, count)
            if name == "static":
                high = scale_ref[l, last, :] * control_ref[l, last, :]
                low = scale_ref[l, first, :] * control_ref[l, first, :]
            else:
                high, low = refs[name][k, l, last, :], refs[name][k, l, first, :]
            up_ref[l // GROUP, at : at + count, :] = high
            down_ref[l // GROUP, at : at + count, :] = low
            at += count


def window_kernel(
    level_ref,
    received_ref,
    inner_ref,
    outer_ref,
    control_ref,
    scale_ref,
    coefs_ref,
    weight_ref,
    innov_ref,
    send_ref,
    grad_ref,
    inner_out_ref,
    outer_out_ref,
    sums_ref,
    low_ref,
    high_ref,
    levels_ref,
    levels_sem,
):
    tiles = received_ref.shape[0]
    levels, rows, nlon = control_ref.shape
    ring = rows + SUB
    halves = nlon // LANES
    refs = {"coefs": coefs_ref, "obs_weight": weight_ref, "innovation": innov_ref}
    copy = pltpu.make_async_copy(level_ref, levels_ref, levels_sem)
    copy.start()
    even = lax.axis_index("tile") % 2 == 0

    @pl.when(even)
    def _():
        low_ref[...] = outer_ref[...]
        high_ref[...] = inner_ref[...]

    @pl.when(jnp.logical_not(even))
    def _():
        low_ref[...] = inner_ref[...]
        high_ref[...] = outer_ref[...]

    sums_ref[...] = jnp.zeros_like(sums_ref)
    copy.wait()
    for d, tile in enumerate(order(tiles)):
        sums_ref[levels_ref[tile]] += received_ref[d]

    above = sublane((SUB, nlon)) < HALO

    def low_rows(g, at, count):
        start = max(at + count - SUB, 0)
        block = low_ref[g, start : start + SUB, :]
        shift = SUB - (at + count - start)
        return pltpu.roll(block, shift, 0) if shift else block

    def high_rows(g, at):
        start = min(at, PACKED - SUB)
        block = high_ref[g, start : start + SUB, :]
        return pltpu.roll(block, SUB - (at - start), 0) if at > start else block

    def level(g, i):
        l = g * GROUP + i
        fields = {}
        at = i * LEVEL_ROWS
        for name, k, count in packed_fields():
            inner = scale_ref[l] * control_ref[l] if name == "static" else refs[name][k, l]
            edge = jnp.where(above, high_rows(g, at), low_rows(g, at, count))
            fields[name, k] = jnp.concatenate([inner, edge], axis=0)
            at += count
        c0, c1, c2, c3 = (fields["coefs", k] for k in range(4))
        rest = 1.0 - (c0 + c1 + c2 + c3)

        sums = []
        for h in range(halves):
            edge = halves * rows + h * SUB
            sums.append(
                jnp.concatenate(
                    [sums_ref[l, h * rows : (h + 1) * rows, :], sums_ref[l, edge : edge + SUB, :]],
                    axis=0,
                )
            )
        state = fields["static", 0] + jnp.concatenate(sums, axis=1)
        weighted = []
        for section in range(STEPS):
            state = (
                rest * state
                + c0 * pltpu.roll(state, ring - 1, 0)
                + c1 * pltpu.roll(state, 1, 0)
                + c2 * pltpu.roll(state, nlon - 1, 1)
                + c3 * pltpu.roll(state, 1, 1)
            )
            if section < SPILL:
                weighted.append(weight_ref[section, l] * (state[:rows] - innov_ref[section, l]))
            else:
                weighted.append(
                    fields["obs_weight", section] * (state - fields["innovation", section])
                )
        adjoint = weighted[STEPS - 1]
        for left in range(STEPS - 1, -1, -1):
            if left + 1 == SPILL:
                adjoint = jnp.concatenate(
                    [adjoint[:rows], jnp.zeros((SUB, nlon), jnp.float32)], axis=0
                )
            adjoint = (
                rest * adjoint
                + pltpu.roll(c0 * adjoint, 1, 0)
                + pltpu.roll(c1 * adjoint, ring - 1, 0)
                + pltpu.roll(c2 * adjoint, 1, 1)
                + pltpu.roll(c3 * adjoint, nlon - 1, 1)
            )
            if left > SPILL:
                adjoint = adjoint + weighted[left - 1]
            elif left > 0:
                adjoint = jnp.concatenate(
                    [adjoint[:rows] + weighted[left - 1], adjoint[rows:]], axis=0
                )
        grad_ref[l] = adjoint
        above_rows, below_rows = adjoint[rows : rows + SPILL], adjoint[ring - SPILL :]
        spot = slice(i * SPILL, (i + 1) * SPILL)
        inner_out_ref[g, spot, :] = jnp.where(even, above_rows, below_rows)
        outer_out_ref[g, spot, :] = jnp.where(even, below_rows, above_rows)

    for l in range(levels):
        level(l // GROUP, l % GROUP)
    row = sublane((SUB, LANES))
    for e, tile in enumerate(order(tiles)):
        at = levels_ref[tile]
        for h in range(0, halves, 2):
            spilled = grad_ref[at, rows:ring, h * LANES : (h + 1) * LANES]
            if h + 1 < halves:
                block = grad_ref[at, rows:ring, (h + 1) * LANES : (h + 2) * LANES]
                middle = jnp.where(
                    row < 2 * SPILL, pltpu.roll(block, SPILL, 0), pltpu.roll(block, SUB - SPILL, 0)
                )
                outer = (row < SPILL) | (row >= SUB - SPILL)
                spilled = jnp.where(outer, spilled, middle)
            start = halves * rows + h // 2 * SUB
            send_ref[e, start : start + SUB, :] = spilled
        for h in range(halves):
            lanes = slice(h * LANES, (h + 1) * LANES)
            send_ref[e, h * rows : (h + 1) * rows, :] = grad_ref[at, 0:rows, lanes]


def member_update_kernel(
    lat_ref,
    lon_ref,
    perts_ref,
    incoming_ref,
    control_ref,
    inner_ref,
    outer_ref,
    tile_grad_ref,
    static_ref,
    scale_ref,
    out_ref,
    static_out_ref,
    field_ref,
):
    tiles = incoming_ref.shape[0]
    blocks, nlat, nlon = control_ref.shape
    rows = nlat // tiles
    halves = nlon // LANES
    half_row = sublane((SUB, LANES))
    position = {tile: p for p, tile in enumerate(order(tiles))}
    for h in range(halves):
        lanes = slice(h * LANES, (h + 1) * LANES)
        start = halves * rows + h // 2 * SUB
        inset = h % 2 * SPILL

        def spill(s, above):
            block = incoming_ref[position[s], start : start + SUB, :]
            if inset:
                block = pltpu.roll(block, SUB - inset if above else inset, 0)
            keep = half_row < SPILL if above else half_row >= SUB - SPILL
            return jnp.where(keep, block, 0.0)

        for s in range(tiles):
            piece = incoming_ref[position[s], h * rows : (h + 1) * rows, :]
            parts = [piece[t * SUB : (t + 1) * SUB] for t in range(rows // SUB)]
            if s > 0:
                parts[0] = parts[0] + spill(s - 1, True)
            if s < tiles - 1:
                parts[-1] = parts[-1] + spill(s + 1, False)
            field_ref[s * rows : (s + 1) * rows, lanes] = jnp.concatenate(parts, axis=0)
    for b in range(blocks):
        weighted = (perts_ref[b].astype(jnp.float32) * field_ref[...]).astype(jnp.bfloat16)
        adjoint_lat = lax.dot_general(
            lat_ref[...], weighted, (((0,), (0,)), ((), ())), preferred_element_type=jnp.float32
        ).astype(jnp.bfloat16)
        member_grad = jnp.dot(adjoint_lat, lon_ref[...], preferred_element_type=jnp.float32)
        control = control_ref[b]
        out_ref[b] = control - STEP_SIZE * (control + member_grad)

    row = sublane((SUB, nlon))
    even = lax.axis_index("tile") % 2 == 0
    for l in range(static_ref.shape[0]):
        at = l % GROUP * SPILL
        inner, outer = inner_ref[l // GROUP, 0:SUB, :], outer_ref[l // GROUP, 0:SUB, :]
        block = jnp.where(even, outer, inner)
        above = jnp.where(row < SPILL, pltpu.roll(block, SUB - at, 0) if at else block, 0.0)
        block = jnp.where(even, inner, outer)
        shift = (SUB - SPILL - at) % SUB
        below = jnp.where(
            row >= SUB - SPILL, pltpu.roll(block, shift, 0) if shift else block, 0.0
        )
        parts = [tile_grad_ref[l, t * SUB : (t + 1) * SUB, :] for t in range(rows // SUB)]
        parts[0] = parts[0] + above
        parts[-1] = parts[-1] + below
        gradient = jnp.concatenate(parts, axis=0)
        static = static_ref[l]
        static_out_ref[l] = static - STEP_SIZE * (static + scale_ref[l] * gradient)


def whole_local(
    level_map, loc_lat, loc_lon, ens_perts, ens_control,
    static_control, static_scale, coefs, obs_weight, innovation,
):
    tiles = lax.axis_size("tile")
    levels, rows, nlon = static_control.shape
    halves = nlon // LANES

    def exchanged_pairs(inner, outer):
        pairs = [[(i, i + 1) for i in range(first, tiles - 1, 2)] for first in (0, 1)]
        both = [pair + [(b, a) for a, b in pair] for pair in pairs]
        return lax.ppermute(inner, "tile", both[0]), lax.ppermute(outer, "tile", both[1])

    def swapped(pieces):
        return lax.all_to_all(
            pieces, "tile", split_axis=0, concat_axis=0, tiled=True,
            axis_index_groups=[order(tiles)],
        )

    def array(*shape):
        return jax.ShapeDtypeStruct(shape, jnp.float32)

    first_shape = (tiles, halves * (rows + SUB), LANES)
    pieces = pl.pallas_call(
        lambda *refs: member_sum_kernel(tiles, *refs),
        out_shape=array(*first_shape),
        in_specs=vmem(4),
        out_specs=vmem(1)[0],
        name="member_sum",
    )(loc_lat, loc_lon, ens_perts, ens_control)
    received = swapped(pieces)

    packed = array(levels // GROUP, PACKED, nlon)
    inner, outer = pl.pallas_call(
        pack_kernel,
        out_shape=(packed, packed),
        in_specs=vmem(5),
        out_specs=tuple(vmem(2)),
        compiler_params=params(8),
        name="pack",
    )(static_control, static_scale, coefs, obs_weight, innovation)
    inner, outer = exchanged_pairs(inner, outer)

    spilled = array(levels // GROUP, GROUP * SPILL, nlon)
    send, tile_grad, inner, outer = pl.pallas_call(
        window_kernel,
        out_shape=(
            array(tiles, halves * rows + -(-halves // 2) * SUB, LANES),
            array(levels, rows + SUB, nlon),
            spilled,
            spilled,
        ),
        in_specs=vmem(9),
        out_specs=tuple(vmem(4)),
        scratch_shapes=[
            pltpu.VMEM((levels,) + first_shape[1:], jnp.float32),
            pltpu.VMEM(packed.shape, jnp.float32),
            pltpu.VMEM(packed.shape, jnp.float32),
            pltpu.SMEM(level_map.shape, jnp.int32),
            pltpu.SemaphoreType.DMA(()),
        ],
        compiler_params=params(8),
        name="window",
    )(level_map, received, inner, outer, static_control, static_scale, coefs, obs_weight, innovation)
    incoming = swapped(send)
    inner, outer = exchanged_pairs(inner, outer)

    return pl.pallas_call(
        member_update_kernel,
        out_shape=(array(*ens_control.shape), array(*static_control.shape)),
        in_specs=vmem(10),
        out_specs=tuple(vmem(2)),
        scratch_shapes=[pltpu.VMEM(ens_control.shape[1:], jnp.float32)],
        compiler_params=params(8),
        name="member_update",
    )(
        loc_lat, loc_lon, ens_perts, incoming, ens_control,
        inner, outer, tile_grad, static_control, static_scale,
    )


def exchanged(block, axis):
    count = lax.axis_size("tile")
    forward = [(i, i + 1) for i in range(count - 1)]
    backward = [(target, source) for source, target in forward]
    last = block.shape[axis] - 1
    low = lax.ppermute(lax.slice_in_dim(block, last, last + 1, axis=axis), "tile", forward)
    high = lax.ppermute(lax.slice_in_dim(block, 0, 1, axis=axis), "tile", backward)
    return jnp.concatenate([low, block, high], axis=axis)


def forward_step(state, coeffs):
    padded = exchanged(state, 1)
    return (
        state
        + coeffs[0] * (padded[:, 2:] - state)
        + coeffs[1] * (padded[:, :-2] - state)
        + coeffs[2] * (jnp.roll(state, -1, 2) - state)
        + coeffs[3] * (jnp.roll(state, 1, 2) - state)
    )


def adjoint_step(adjoint, coeffs):
    coef_sum = coeffs[0] + coeffs[1] + coeffs[2] + coeffs[3]
    padded = exchanged(jnp.stack([coeffs[0] * adjoint, coeffs[1] * adjoint]), 2)
    return (
        (1.0 - coef_sum) * adjoint
        + padded[0][:, :-2]
        + padded[1][:, 2:]
        + jnp.roll(coeffs[2] * adjoint, 1, 2)
        + jnp.roll(coeffs[3] * adjoint, -1, 2)
    )


def any_local(
    level_map, loc_lat, loc_lon, ens_perts, ens_control,
    static_control, static_scale, coefs, obs_weight, innovation,
):
    tiles = lax.axis_size("tile")
    level_ids = jnp.arange(static_control.shape[0], dtype=jnp.int32)
    level_onehot = (level_map[:, None] == level_ids[None, :]).astype(jnp.float32)
    lat_smoothed = jnp.einsum(
        "ij,bjk->bik", loc_lat, ens_control.astype(jnp.bfloat16),
        preferred_element_type=jnp.float32,
    ).astype(jnp.bfloat16)
    member_field = jnp.einsum(
        "bij,kj->bik", lat_smoothed, loc_lon, preferred_element_type=jnp.float32
    )
    partial_value = jnp.sum(ens_perts.astype(jnp.float32) * member_field, axis=0)
    pieces = partial_value.reshape(tiles, -1, partial_value.shape[1])
    received = lax.all_to_all(pieces, "tile", split_axis=0, concat_axis=0, tiled=True)
    ens_incr = jnp.einsum("dl,dij->lij", level_onehot, received, precision=lax.Precision.HIGHEST)
    state = static_scale * static_control + ens_incr
    weighted = []
    for section in range(STEPS):
        state = forward_step(state, coefs)
        weighted.append(obs_weight[section] * (state - innovation[section]))
    adjoint = weighted[STEPS - 1]
    for section in range(STEPS - 2, -1, -1):
        adjoint = adjoint_step(adjoint, coefs) + weighted[section]
    gradient = adjoint_step(adjoint, coefs)
    static_final = static_control - STEP_SIZE * (static_control + static_scale * gradient)
    outgoing = jnp.take(gradient, level_map, axis=0)
    incoming = lax.all_to_all(outgoing, "tile", split_axis=0, concat_axis=0, tiled=True)
    grad_field = incoming.reshape(-1, incoming.shape[2])
    weighted_grad = (ens_perts.astype(jnp.float32) * grad_field[None]).astype(jnp.bfloat16)
    adjoint_lat = jnp.einsum(
        "ji,bjk->bik", loc_lat, weighted_grad, preferred_element_type=jnp.float32
    ).astype(jnp.bfloat16)
    member_grad = jnp.einsum("bij,jk->bik", adjoint_lat, loc_lon, preferred_element_type=jnp.float32)
    return ens_control - STEP_SIZE * (ens_control + member_grad), static_final


def local(*args):
    levels, rows, nlon = args[5].shape
    whole = rows % SUB == 0 and nlon % LANES == 0 and levels % GROUP == 0
    return (whole_local if whole else any_local)(*args)


def solution(mesh):
    in_specs = (
        P(),
        P(),
        P(),
        P(("groups", "tile"), None, None),
        P(("groups", "tile"), None, None),
        P("groups", "tile", None),
        P("groups", "tile", None),
        P(None, "groups", "tile", None),
        P(None, "groups", "tile", None),
        P(None, "groups", "tile", None),
    )
    out_specs = (P(("groups", "tile"), None, None), P("groups", "tile", None))
    return jax.shard_map(local, mesh=mesh, in_specs=in_specs, out_specs=out_specs, check_vma=False)
```

```python
import jax
import jax.numpy as jnp
from jax import lax
from jax.experimental import pallas as pl
from jax.experimental.pallas import tpu as pltpu
from jax.sharding import PartitionSpec as P

STEPS = 3
LANES = 128
SUB = 8
STEP_SIZE = 0.15
GROUP = 4

SPILL = 2
HALO = 2 * STEPS - SPILL


def packed_fields():
    fields = [("static", 0, HALO)]
    fields += [("coefs", k, HALO - 1) for k in range(4)]
    for section in range(SPILL, STEPS):
        fields += [(name, section, section + 1 - SPILL) for name in ("obs_weight", "innovation")]
    return fields


LEVEL_ROWS = sum(rows for _, _, rows in packed_fields())
PACKED = GROUP * LEVEL_ROWS


def vmem(count):
    return [pl.BlockSpec(memory_space=pltpu.VMEM)] * count


def params(mebibytes):
    return pltpu.CompilerParams(vmem_limit_bytes=mebibytes << 20)


def order(tiles):
    quarters = [list(range(q * tiles // 4, (q + 1) * tiles // 4))[::-1] for q in (2, 0, 1, 3)]
    return sum(quarters, [])


def sublane(shape):
    return lax.broadcasted_iota(jnp.int32, shape, 0)


def member_sum_kernel(tiles, lat_ref, lon_ref, perts_ref, control_ref, out_ref):
    blocks, nlat, nlon = control_ref.shape
    rows = nlat // tiles
    halves = nlon // LANES
    total = None
    for b in range(blocks):
        smoothed = jnp.dot(
            lat_ref[...], control_ref[b].astype(jnp.bfloat16), preferred_element_type=jnp.float32
        ).astype(jnp.bfloat16)
        field = lax.dot_general(
            smoothed, lon_ref[...], (((1,), (1,)), ((), ())), preferred_element_type=jnp.float32
        )
        term = perts_ref[b].astype(jnp.float32) * field
        total = term if total is None else total + term
    first = sublane((SUB, LANES)) < HALO
    edge = jnp.zeros((SUB, LANES), jnp.float32)
    for e, tile in enumerate(order(tiles)):
        start = tile * rows
        end = start + rows
        for h in range(halves):
            lanes = slice(h * LANES, (h + 1) * LANES)
            above = total[end : end + SUB, lanes] if end < nlat else edge
            below = total[start - SUB : start, lanes] if start > 0 else edge
            out_ref[e, h * rows : (h + 1) * rows, :] = total[start:end, lanes]
            at = halves * rows + h * SUB
            out_ref[e, at : at + SUB, :] = jnp.where(first, above, below)


def pack_kernel(control_ref, scale_ref, coefs_ref, weight_ref, innov_ref, inner_ref, outer_ref):
    even = lax.axis_index("tile") % 2 == 0

    @pl.when(even)
    def _():
        pack(control_ref, scale_ref, coefs_ref, weight_ref, innov_ref, inner_ref, outer_ref)

    @pl.when(jnp.logical_not(even))
    def _():
        pack(control_ref, scale_ref, coefs_ref, weight_ref, innov_ref, outer_ref, inner_ref)


def pack(control_ref, scale_ref, coefs_ref, weight_ref, innov_ref, up_ref, down_ref):
    refs = {"coefs": coefs_ref, "obs_weight": weight_ref, "innovation": innov_ref}
    levels, rows, _ = control_ref.shape
    for l in range(levels):
        at = l % GROUP * LEVEL_ROWS
        for name, k, count in packed_fields():
            last, first = slice(rows - count, rows), slice(0, count)
            if name == "static":
                high = scale_ref[l, last, :] * control_ref[l, last, :]
                low = scale_ref[l, first, :] * control_ref[l, first, :]
            else:
                high, low = refs[name][k, l, last, :], refs[name][k, l, first, :]
            up_ref[l // GROUP, at : at + count, :] = high
            down_ref[l // GROUP, at : at + count, :] = low
            at += count


def window_kernel(
    level_ref,
    received_ref,
    inner_ref,
    outer_ref,
    control_ref,
    scale_ref,
    coefs_ref,
    weight_ref,
    innov_ref,
    send_ref,
    grad_ref,
    inner_out_ref,
    outer_out_ref,
    sums_ref,
    low_ref,
    high_ref,
):
    tiles = received_ref.shape[0]
    levels, rows, nlon = control_ref.shape
    ring = rows + SUB
    halves = nlon // LANES
    refs = {"coefs": coefs_ref, "obs_weight": weight_ref, "innovation": innov_ref}
    even = lax.axis_index("tile") % 2 == 0

    @pl.when(even)
    def _():
        low_ref[...] = outer_ref[...]
        high_ref[...] = inner_ref[...]

    @pl.when(jnp.logical_not(even))
    def _():
        low_ref[...] = inner_ref[...]
        high_ref[...] = outer_ref[...]

    sums_ref[...] = jnp.zeros_like(sums_ref)
    for d, tile in enumerate(order(tiles)):
        sums_ref[level_ref[tile]] += received_ref[d]

    above = sublane((SUB, nlon)) < HALO

    def low_rows(g, at, count):
        start = max(at + count - SUB, 0)
        block = low_ref[g, start : start + SUB, :]
        shift = SUB - (at + count - start)
        return pltpu.roll(block, shift, 0) if shift else block

    def high_rows(g, at):
        start = min(at, PACKED - SUB)
        block = high_ref[g, start : start + SUB, :]
        return pltpu.roll(block, SUB - (at - start), 0) if at > start else block

    def level(g, i):
        l = g * GROUP + i
        fields = {}
        at = i * LEVEL_ROWS
        for name, k, count in packed_fields():
            inner = scale_ref[l] * control_ref[l] if name == "static" else refs[name][k, l]
            edge = jnp.where(above, high_rows(g, at), low_rows(g, at, count))
            fields[name, k] = jnp.concatenate([inner, edge], axis=0)
            at += count
        c0, c1, c2, c3 = (fields["coefs", k] for k in range(4))
        rest = 1.0 - (c0 + c1 + c2 + c3)

        sums = []
        for h in range(halves):
            edge = halves * rows + h * SUB
            sums.append(
                jnp.concatenate(
                    [sums_ref[l, h * rows : (h + 1) * rows, :], sums_ref[l, edge : edge + SUB, :]],
                    axis=0,
                )
            )
        state = fields["static", 0] + jnp.concatenate(sums, axis=1)
        weighted = []
        for section in range(STEPS):
            state = (
                rest * state
                + c0 * pltpu.roll(state, ring - 1, 0)
                + c1 * pltpu.roll(state, 1, 0)
                + c2 * pltpu.roll(state, nlon - 1, 1)
                + c3 * pltpu.roll(state, 1, 1)
            )
            if section < SPILL:
                weighted.append(weight_ref[section, l] * (state[:rows] - innov_ref[section, l]))
            else:
                weighted.append(
                    fields["obs_weight", section] * (state - fields["innovation", section])
                )
        adjoint = weighted[STEPS - 1]
        for left in range(STEPS - 1, -1, -1):
            if left + 1 == SPILL:
                adjoint = jnp.concatenate(
                    [adjoint[:rows], jnp.zeros((SUB, nlon), jnp.float32)], axis=0
                )
            adjoint = (
                rest * adjoint
                + pltpu.roll(c0 * adjoint, 1, 0)
                + pltpu.roll(c1 * adjoint, ring - 1, 0)
                + pltpu.roll(c2 * adjoint, 1, 1)
                + pltpu.roll(c3 * adjoint, nlon - 1, 1)
            )
            if left > SPILL:
                adjoint = adjoint + weighted[left - 1]
            elif left > 0:
                adjoint = jnp.concatenate(
                    [adjoint[:rows] + weighted[left - 1], adjoint[rows:]], axis=0
                )
        grad_ref[l] = adjoint
        above_rows, below_rows = adjoint[rows : rows + SPILL], adjoint[ring - SPILL :]
        spot = slice(i * SPILL, (i + 1) * SPILL)
        inner_out_ref[g, spot, :] = jnp.where(even, above_rows, below_rows)
        outer_out_ref[g, spot, :] = jnp.where(even, below_rows, above_rows)

    for l in range(levels):
        level(l // GROUP, l % GROUP)
    row = sublane((SUB, LANES))
    for e, tile in enumerate(order(tiles)):
        at = level_ref[tile]
        for h in range(0, halves, 2):
            spilled = grad_ref[at, rows:ring, h * LANES : (h + 1) * LANES]
            if h + 1 < halves:
                block = grad_ref[at, rows:ring, (h + 1) * LANES : (h + 2) * LANES]
                middle = jnp.where(
                    row < 2 * SPILL, pltpu.roll(block, SPILL, 0), pltpu.roll(block, SUB - SPILL, 0)
                )
                outer = (row < SPILL) | (row >= SUB - SPILL)
                spilled = jnp.where(outer, spilled, middle)
            start = halves * rows + h // 2 * SUB
            send_ref[e, start : start + SUB, :] = spilled
        for h in range(halves):
            lanes = slice(h * LANES, (h + 1) * LANES)
            send_ref[e, h * rows : (h + 1) * rows, :] = grad_ref[at, 0:rows, lanes]


def member_update_kernel(
    lat_ref,
    lon_ref,
    perts_ref,
    incoming_ref,
    control_ref,
    out_ref,
    field_ref,
):
    tiles = incoming_ref.shape[0]
    blocks, nlat, nlon = control_ref.shape
    rows = nlat // tiles
    halves = nlon // LANES
    half_row = sublane((SUB, LANES))
    position = {tile: p for p, tile in enumerate(order(tiles))}
    for h in range(halves):
        lanes = slice(h * LANES, (h + 1) * LANES)
        start = halves * rows + h // 2 * SUB
        inset = h % 2 * SPILL

        def spill(s, above):
            block = incoming_ref[position[s], start : start + SUB, :]
            if inset:
                block = pltpu.roll(block, SUB - inset if above else inset, 0)
            keep = half_row < SPILL if above else half_row >= SUB - SPILL
            return jnp.where(keep, block, 0.0)

        for s in range(tiles):
            piece = incoming_ref[position[s], h * rows : (h + 1) * rows, :]
            parts = [piece[t * SUB : (t + 1) * SUB] for t in range(rows // SUB)]
            if s > 0:
                parts[0] = parts[0] + spill(s - 1, True)
            if s < tiles - 1:
                parts[-1] = parts[-1] + spill(s + 1, False)
            field_ref[s * rows : (s + 1) * rows, lanes] = jnp.concatenate(parts, axis=0)
    for b in range(blocks):
        weighted = (perts_ref[b].astype(jnp.float32) * field_ref[...]).astype(jnp.bfloat16)
        adjoint_lat = lax.dot_general(
            lat_ref[...], weighted, (((0,), (0,)), ((), ())), preferred_element_type=jnp.float32
        ).astype(jnp.bfloat16)
        member_grad = jnp.dot(adjoint_lat, lon_ref[...], preferred_element_type=jnp.float32)
        control = control_ref[b]
        out_ref[b] = control - STEP_SIZE * (control + member_grad)


def static_update_kernel(
    inner_ref, outer_ref, tile_grad_ref, static_ref, scale_ref, static_out_ref
):
    rows, nlon = static_ref.shape[1:]
    row = sublane((SUB, nlon))
    even = lax.axis_index("tile") % 2 == 0
    for l in range(static_ref.shape[0]):
        at = l % GROUP * SPILL
        inner, outer = inner_ref[l // GROUP, 0:SUB, :], outer_ref[l // GROUP, 0:SUB, :]
        block = jnp.where(even, outer, inner)
        above = jnp.where(row < SPILL, pltpu.roll(block, SUB - at, 0) if at else block, 0.0)
        block = jnp.where(even, inner, outer)
        shift = (SUB - SPILL - at) % SUB
        below = jnp.where(
            row >= SUB - SPILL, pltpu.roll(block, shift, 0) if shift else block, 0.0
        )
        parts = [tile_grad_ref[l, t * SUB : (t + 1) * SUB, :] for t in range(rows // SUB)]
        parts[0] = parts[0] + above
        parts[-1] = parts[-1] + below
        gradient = jnp.concatenate(parts, axis=0)
        static = static_ref[l]
        static_out_ref[l] = static - STEP_SIZE * (static + scale_ref[l] * gradient)


def whole_local(
    level_map, loc_lat, loc_lon, ens_perts, ens_control,
    static_control, static_scale, coefs, obs_weight, innovation,
):
    tiles = lax.axis_size("tile")
    levels, rows, nlon = static_control.shape
    halves = nlon // LANES

    def exchanged_pairs(inner, outer):
        pairs = [[(i, i + 1) for i in range(first, tiles - 1, 2)] for first in (0, 1)]
        both = [pair + [(b, a) for a, b in pair] for pair in pairs]
        return lax.ppermute(inner, "tile", both[0]), lax.ppermute(outer, "tile", both[1])

    def swapped(pieces):
        return lax.all_to_all(
            pieces, "tile", split_axis=0, concat_axis=0, tiled=True,
            axis_index_groups=[order(tiles)],
        )

    def array(*shape):
        return jax.ShapeDtypeStruct(shape, jnp.float32)

    first_shape = (tiles, halves * (rows + SUB), LANES)
    pieces = pl.pallas_call(
        lambda *refs: member_sum_kernel(tiles, *refs),
        out_shape=array(*first_shape),
        in_specs=vmem(4),
        out_specs=vmem(1)[0],
        name="member_sum",
    )(loc_lat, loc_lon, ens_perts, ens_control)
    received = swapped(pieces)

    packed = array(levels // GROUP, PACKED, nlon)
    inner, outer = pl.pallas_call(
        pack_kernel,
        out_shape=(packed, packed),
        in_specs=vmem(5),
        out_specs=tuple(vmem(2)),
        compiler_params=params(8),
        name="pack",
    )(static_control, static_scale, coefs, obs_weight, innovation)
    inner, outer = exchanged_pairs(inner, outer)

    spilled = array(levels // GROUP, GROUP * SPILL, nlon)
    send, tile_grad, inner, outer = pl.pallas_call(
        window_kernel,
        out_shape=(
            array(tiles, halves * rows + -(-halves // 2) * SUB, LANES),
            array(levels, rows + SUB, nlon),
            spilled,
            spilled,
        ),
        in_specs=[pl.BlockSpec(memory_space=pltpu.SMEM)] + vmem(8),
        out_specs=tuple(vmem(4)),
        scratch_shapes=[
            pltpu.VMEM((levels,) + first_shape[1:], jnp.float32),
            pltpu.VMEM(packed.shape, jnp.float32),
            pltpu.VMEM(packed.shape, jnp.float32),
        ],
        compiler_params=params(8),
        name="window",
    )(level_map, received, inner, outer, static_control, static_scale, coefs, obs_weight, innovation)
    incoming = swapped(send)
    inner, outer = exchanged_pairs(inner, outer)

    static_final = pl.pallas_call(
        static_update_kernel,
        out_shape=array(*static_control.shape),
        in_specs=vmem(5),
        out_specs=vmem(1)[0],
        compiler_params=params(8),
        name="static_update",
    )(inner, outer, tile_grad, static_control, static_scale)
    ens_final = pl.pallas_call(
        member_update_kernel,
        out_shape=array(*ens_control.shape),
        in_specs=vmem(5),
        out_specs=vmem(1)[0],
        scratch_shapes=[pltpu.VMEM(ens_control.shape[1:], jnp.float32)],
        compiler_params=params(8),
        name="member_update",
    )(loc_lat, loc_lon, ens_perts, incoming, ens_control)
    return ens_final, static_final


def exchanged(block, axis):
    count = lax.axis_size("tile")
    forward = [(i, i + 1) for i in range(count - 1)]
    backward = [(target, source) for source, target in forward]
    last = block.shape[axis] - 1
    low = lax.ppermute(lax.slice_in_dim(block, last, last + 1, axis=axis), "tile", forward)
    high = lax.ppermute(lax.slice_in_dim(block, 0, 1, axis=axis), "tile", backward)
    return jnp.concatenate([low, block, high], axis=axis)


def forward_step(state, coeffs):
    padded = exchanged(state, 1)
    return (
        state
        + coeffs[0] * (padded[:, 2:] - state)
        + coeffs[1] * (padded[:, :-2] - state)
        + coeffs[2] * (jnp.roll(state, -1, 2) - state)
        + coeffs[3] * (jnp.roll(state, 1, 2) - state)
    )


def adjoint_step(adjoint, coeffs):
    coef_sum = coeffs[0] + coeffs[1] + coeffs[2] + coeffs[3]
    padded = exchanged(jnp.stack([coeffs[0] * adjoint, coeffs[1] * adjoint]), 2)
    return (
        (1.0 - coef_sum) * adjoint
        + padded[0][:, :-2]
        + padded[1][:, 2:]
        + jnp.roll(coeffs[2] * adjoint, 1, 2)
        + jnp.roll(coeffs[3] * adjoint, -1, 2)
    )


def any_local(
    level_map, loc_lat, loc_lon, ens_perts, ens_control,
    static_control, static_scale, coefs, obs_weight, innovation,
):
    tiles = lax.axis_size("tile")
    level_ids = jnp.arange(static_control.shape[0], dtype=jnp.int32)
    level_onehot = (level_map[:, None] == level_ids[None, :]).astype(jnp.float32)
    lat_smoothed = jnp.einsum(
        "ij,bjk->bik", loc_lat, ens_control.astype(jnp.bfloat16),
        preferred_element_type=jnp.float32,
    ).astype(jnp.bfloat16)
    member_field = jnp.einsum(
        "bij,kj->bik", lat_smoothed, loc_lon, preferred_element_type=jnp.float32
    )
    partial_value = jnp.sum(ens_perts.astype(jnp.float32) * member_field, axis=0)
    pieces = partial_value.reshape(tiles, -1, partial_value.shape[1])
    received = lax.all_to_all(pieces, "tile", split_axis=0, concat_axis=0, tiled=True)
    ens_incr = jnp.einsum("dl,dij->lij", level_onehot, received, precision=lax.Precision.HIGHEST)
    state = static_scale * static_control + ens_incr
    weighted = []
    for section in range(STEPS):
        state = forward_step(state, coefs)
        weighted.append(obs_weight[section] * (state - innovation[section]))
    adjoint = weighted[STEPS - 1]
    for section in range(STEPS - 2, -1, -1):
        adjoint = adjoint_step(adjoint, coefs) + weighted[section]
    gradient = adjoint_step(adjoint, coefs)
    static_final = static_control - STEP_SIZE * (static_control + static_scale * gradient)
    outgoing = jnp.take(gradient, level_map, axis=0)
    incoming = lax.all_to_all(outgoing, "tile", split_axis=0, concat_axis=0, tiled=True)
    grad_field = incoming.reshape(-1, incoming.shape[2])
    weighted_grad = (ens_perts.astype(jnp.float32) * grad_field[None]).astype(jnp.bfloat16)
    adjoint_lat = jnp.einsum(
        "ji,bjk->bik", loc_lat, weighted_grad, preferred_element_type=jnp.float32
    ).astype(jnp.bfloat16)
    member_grad = jnp.einsum("bij,jk->bik", adjoint_lat, loc_lon, preferred_element_type=jnp.float32)
    return ens_control - STEP_SIZE * (ens_control + member_grad), static_final


def local(*args):
    levels, rows, nlon = args[5].shape
    whole = rows % SUB == 0 and nlon % LANES == 0 and levels % GROUP == 0
    return (whole_local if whole else any_local)(*args)


def solution(mesh):
    in_specs = (
        P(),
        P(),
        P(),
        P(("groups", "tile"), None, None),
        P(("groups", "tile"), None, None),
        P("groups", "tile", None),
        P("groups", "tile", None),
        P(None, "groups", "tile", None),
        P(None, "groups", "tile", None),
        P(None, "groups", "tile", None),
    )
    out_specs = (P(("groups", "tile"), None, None), P("groups", "tile", None))
    return jax.shard_map(local, mesh=mesh, in_specs=in_specs, out_specs=out_specs, check_vma=False)
```

```python
import jax
import jax.numpy as jnp
from jax import lax
from jax.experimental import pallas as pl
from jax.experimental.pallas import tpu as pltpu
from jax.sharding import PartitionSpec as P

STEPS = 3
LANES = 128
SUB = 8
STEP_SIZE = 0.15
GROUP = 4

SPILL = 2
HALO = 2 * STEPS - SPILL


def packed_fields():
    fields = [("static", 0, HALO)]
    fields += [("coefs", k, HALO - 1) for k in range(4)]
    for section in range(SPILL, STEPS):
        fields += [(name, section, section + 1 - SPILL) for name in ("obs_weight", "innovation")]
    return fields


LEVEL_ROWS = sum(rows for _, _, rows in packed_fields())
PACKED = GROUP * LEVEL_ROWS


def vmem(count):
    return [pl.BlockSpec(memory_space=pltpu.VMEM)] * count


def params(mebibytes):
    return pltpu.CompilerParams(vmem_limit_bytes=mebibytes << 20)


def order(tiles):
    quarters = [list(range(q * tiles // 4, (q + 1) * tiles // 4))[::-1] for q in (2, 0, 1, 3)]
    return sum(quarters, [])


def sublane(shape):
    return lax.broadcasted_iota(jnp.int32, shape, 0)


def member_sum_kernel(tiles, control_ref, lat_ref, lon_ref, perts_ref, out_ref):
    blocks, nlat, nlon = control_ref.shape
    rows = nlat // tiles
    halves = nlon // LANES
    total = None
    for b in range(blocks):
        smoothed = jnp.dot(
            lat_ref[...], control_ref[b].astype(jnp.bfloat16), preferred_element_type=jnp.float32
        ).astype(jnp.bfloat16)
        field = lax.dot_general(
            smoothed, lon_ref[...], (((1,), (1,)), ((), ())), preferred_element_type=jnp.float32
        )
        term = perts_ref[b].astype(jnp.float32) * field
        total = term if total is None else total + term
    first = sublane((SUB, LANES)) < HALO
    edge = jnp.zeros((SUB, LANES), jnp.float32)
    for e, tile in enumerate(order(tiles)):
        start = tile * rows
        end = start + rows
        for h in range(halves):
            lanes = slice(h * LANES, (h + 1) * LANES)
            above = total[end : end + SUB, lanes] if end < nlat else edge
            below = total[start - SUB : start, lanes] if start > 0 else edge
            out_ref[e, h * rows : (h + 1) * rows, :] = total[start:end, lanes]
            at = halves * rows + h * SUB
            out_ref[e, at : at + SUB, :] = jnp.where(first, above, below)


def pack_kernel(control_ref, scale_ref, coefs_ref, weight_ref, innov_ref, inner_ref, outer_ref):
    even = lax.axis_index("tile") % 2 == 0

    @pl.when(even)
    def _():
        pack(control_ref, scale_ref, coefs_ref, weight_ref, innov_ref, inner_ref, outer_ref)

    @pl.when(jnp.logical_not(even))
    def _():
        pack(control_ref, scale_ref, coefs_ref, weight_ref, innov_ref, outer_ref, inner_ref)


def pack(control_ref, scale_ref, coefs_ref, weight_ref, innov_ref, up_ref, down_ref):
    refs = {"coefs": coefs_ref, "obs_weight": weight_ref, "innovation": innov_ref}
    levels, rows, _ = control_ref.shape
    for l in range(levels):
        at = l % GROUP * LEVEL_ROWS
        for name, k, count in packed_fields():
            last, first = slice(rows - count, rows), slice(0, count)
            if name == "static":
                high = scale_ref[l, last, :] * control_ref[l, last, :]
                low = scale_ref[l, first, :] * control_ref[l, first, :]
            else:
                high, low = refs[name][k, l, last, :], refs[name][k, l, first, :]
            up_ref[l // GROUP, at : at + count, :] = high
            down_ref[l // GROUP, at : at + count, :] = low
            at += count


def window_kernel(
    level_ref,
    received_ref,
    inner_ref,
    outer_ref,
    control_ref,
    scale_ref,
    coefs_ref,
    weight_ref,
    innov_ref,
    send_ref,
    grad_ref,
    inner_out_ref,
    outer_out_ref,
    sums_ref,
    low_ref,
    high_ref,
):
    tiles = received_ref.shape[0]
    levels, rows, nlon = control_ref.shape
    ring = rows + SUB
    halves = nlon // LANES
    refs = {"coefs": coefs_ref, "obs_weight": weight_ref, "innovation": innov_ref}
    even = lax.axis_index("tile") % 2 == 0

    @pl.when(even)
    def _():
        low_ref[...] = outer_ref[...]
        high_ref[...] = inner_ref[...]

    @pl.when(jnp.logical_not(even))
    def _():
        low_ref[...] = inner_ref[...]
        high_ref[...] = outer_ref[...]

    sums_ref[...] = jnp.zeros_like(sums_ref)
    for d, tile in enumerate(order(tiles)):
        sums_ref[level_ref[tile]] += received_ref[d]

    above = sublane((SUB, nlon)) < HALO

    def low_rows(g, at, count):
        start = max(at + count - SUB, 0)
        block = low_ref[g, start : start + SUB, :]
        shift = SUB - (at + count - start)
        return pltpu.roll(block, shift, 0) if shift else block

    def high_rows(g, at):
        start = min(at, PACKED - SUB)
        block = high_ref[g, start : start + SUB, :]
        return pltpu.roll(block, SUB - (at - start), 0) if at > start else block

    def level(g, i):
        l = g * GROUP + i
        fields = {}
        at = i * LEVEL_ROWS
        for name, k, count in packed_fields():
            inner = scale_ref[l] * control_ref[l] if name == "static" else refs[name][k, l]
            edge = jnp.where(above, high_rows(g, at), low_rows(g, at, count))
            fields[name, k] = jnp.concatenate([inner, edge], axis=0)
            at += count
        c0, c1, c2, c3 = (fields["coefs", k] for k in range(4))
        rest = 1.0 - (c0 + c1 + c2 + c3)

        sums = []
        for h in range(halves):
            edge = halves * rows + h * SUB
            sums.append(
                jnp.concatenate(
                    [sums_ref[l, h * rows : (h + 1) * rows, :], sums_ref[l, edge : edge + SUB, :]],
                    axis=0,
                )
            )
        state = fields["static", 0] + jnp.concatenate(sums, axis=1)
        weighted = []
        for section in range(STEPS):
            state = (
                rest * state
                + c0 * pltpu.roll(state, ring - 1, 0)
                + c1 * pltpu.roll(state, 1, 0)
                + c2 * pltpu.roll(state, nlon - 1, 1)
                + c3 * pltpu.roll(state, 1, 1)
            )
            if section < SPILL:
                weighted.append(weight_ref[section, l] * (state[:rows] - innov_ref[section, l]))
            else:
                weighted.append(
                    fields["obs_weight", section] * (state - fields["innovation", section])
                )
        adjoint = weighted[STEPS - 1]
        for left in range(STEPS - 1, -1, -1):
            if left + 1 == SPILL:
                adjoint = jnp.concatenate(
                    [adjoint[:rows], jnp.zeros((SUB, nlon), jnp.float32)], axis=0
                )
            adjoint = (
                rest * adjoint
                + pltpu.roll(c0 * adjoint, 1, 0)
                + pltpu.roll(c1 * adjoint, ring - 1, 0)
                + pltpu.roll(c2 * adjoint, 1, 1)
                + pltpu.roll(c3 * adjoint, nlon - 1, 1)
            )
            if left > SPILL:
                adjoint = adjoint + weighted[left - 1]
            elif left > 0:
                adjoint = jnp.concatenate(
                    [adjoint[:rows] + weighted[left - 1], adjoint[rows:]], axis=0
                )
        grad_ref[l] = adjoint
        above_rows, below_rows = adjoint[rows : rows + SPILL], adjoint[ring - SPILL :]
        spot = slice(i * SPILL, (i + 1) * SPILL)
        inner_out_ref[g, spot, :] = jnp.where(even, above_rows, below_rows)
        outer_out_ref[g, spot, :] = jnp.where(even, below_rows, above_rows)

    for l in range(levels):
        level(l // GROUP, l % GROUP)
    row = sublane((SUB, LANES))
    for e, tile in enumerate(order(tiles)):
        at = level_ref[tile]
        for h in range(0, halves, 2):
            spilled = grad_ref[at, rows:ring, h * LANES : (h + 1) * LANES]
            if h + 1 < halves:
                block = grad_ref[at, rows:ring, (h + 1) * LANES : (h + 2) * LANES]
                middle = jnp.where(
                    row < 2 * SPILL, pltpu.roll(block, SPILL, 0), pltpu.roll(block, SUB - SPILL, 0)
                )
                outer = (row < SPILL) | (row >= SUB - SPILL)
                spilled = jnp.where(outer, spilled, middle)
            start = halves * rows + h // 2 * SUB
            send_ref[e, start : start + SUB, :] = spilled
        for h in range(halves):
            lanes = slice(h * LANES, (h + 1) * LANES)
            send_ref[e, h * rows : (h + 1) * rows, :] = grad_ref[at, 0:rows, lanes]


def member_update_kernel(
    lat_ref,
    lon_ref,
    perts_ref,
    incoming_ref,
    control_ref,
    inner_ref,
    outer_ref,
    tile_grad_ref,
    static_ref,
    scale_ref,
    out_ref,
    static_out_ref,
    field_ref,
):
    tiles = incoming_ref.shape[0]
    blocks, nlat, nlon = control_ref.shape
    rows = nlat // tiles
    halves = nlon // LANES
    half_row = sublane((SUB, LANES))
    position = {tile: p for p, tile in enumerate(order(tiles))}
    for h in range(halves):
        lanes = slice(h * LANES, (h + 1) * LANES)
        start = halves * rows + h // 2 * SUB
        inset = h % 2 * SPILL

        def spill(s, above):
            block = incoming_ref[position[s], start : start + SUB, :]
            if inset:
                block = pltpu.roll(block, SUB - inset if above else inset, 0)
            keep = half_row < SPILL if above else half_row >= SUB - SPILL
            return jnp.where(keep, block, 0.0)

        for s in range(tiles):
            piece = incoming_ref[position[s], h * rows : (h + 1) * rows, :]
            parts = [piece[t * SUB : (t + 1) * SUB] for t in range(rows // SUB)]
            if s > 0:
                parts[0] = parts[0] + spill(s - 1, True)
            if s < tiles - 1:
                parts[-1] = parts[-1] + spill(s + 1, False)
            field_ref[s * rows : (s + 1) * rows, lanes] = jnp.concatenate(parts, axis=0)
    for b in range(blocks):
        weighted = (perts_ref[b].astype(jnp.float32) * field_ref[...]).astype(jnp.bfloat16)
        adjoint_lat = lax.dot_general(
            lat_ref[...], weighted, (((0,), (0,)), ((), ())), preferred_element_type=jnp.float32
        ).astype(jnp.bfloat16)
        member_grad = jnp.dot(adjoint_lat, lon_ref[...], preferred_element_type=jnp.float32)
        control = control_ref[b]
        out_ref[b] = control - STEP_SIZE * (control + member_grad)

    row = sublane((SUB, nlon))
    even = lax.axis_index("tile") % 2 == 0
    for l in range(static_ref.shape[0]):
        at = l % GROUP * SPILL
        inner, outer = inner_ref[l // GROUP, 0:SUB, :], outer_ref[l // GROUP, 0:SUB, :]
        block = jnp.where(even, outer, inner)
        above = jnp.where(row < SPILL, pltpu.roll(block, SUB - at, 0) if at else block, 0.0)
        block = jnp.where(even, inner, outer)
        shift = (SUB - SPILL - at) % SUB
        below = jnp.where(
            row >= SUB - SPILL, pltpu.roll(block, shift, 0) if shift else block, 0.0
        )
        parts = [tile_grad_ref[l, t * SUB : (t + 1) * SUB, :] for t in range(rows // SUB)]
        parts[0] = parts[0] + above
        parts[-1] = parts[-1] + below
        gradient = jnp.concatenate(parts, axis=0)
        static = static_ref[l]
        static_out_ref[l] = static - STEP_SIZE * (static + scale_ref[l] * gradient)


def whole_local(
    level_map, loc_lat, loc_lon, ens_perts, ens_control,
    static_control, static_scale, coefs, obs_weight, innovation,
):
    tiles = lax.axis_size("tile")
    levels, rows, nlon = static_control.shape
    halves = nlon // LANES

    def exchanged_pairs(inner, outer):
        pairs = [[(i, i + 1) for i in range(first, tiles - 1, 2)] for first in (0, 1)]
        both = [pair + [(b, a) for a, b in pair] for pair in pairs]
        return lax.ppermute(inner, "tile", both[0]), lax.ppermute(outer, "tile", both[1])

    def swapped(pieces):
        return lax.all_to_all(
            pieces, "tile", split_axis=0, concat_axis=0, tiled=True,
            axis_index_groups=[order(tiles)],
        )

    def array(*shape):
        return jax.ShapeDtypeStruct(shape, jnp.float32)

    first_shape = (tiles, halves * (rows + SUB), LANES)
    pieces = pl.pallas_call(
        lambda *refs: member_sum_kernel(tiles, *refs),
        out_shape=array(*first_shape),
        in_specs=vmem(4),
        out_specs=vmem(1)[0],
        name="member_sum",
    )(ens_control, loc_lat, loc_lon, ens_perts)
    received = swapped(pieces)

    packed = array(levels // GROUP, PACKED, nlon)
    inner, outer = pl.pallas_call(
        pack_kernel,
        out_shape=(packed, packed),
        in_specs=vmem(5),
        out_specs=tuple(vmem(2)),
        compiler_params=params(8),
        name="pack",
    )(static_control, static_scale, coefs, obs_weight, innovation)
    inner, outer = exchanged_pairs(inner, outer)

    spilled = array(levels // GROUP, GROUP * SPILL, nlon)
    send, tile_grad, inner, outer = pl.pallas_call(
        window_kernel,
        out_shape=(
            array(tiles, halves * rows + -(-halves // 2) * SUB, LANES),
            array(levels, rows + SUB, nlon),
            spilled,
            spilled,
        ),
        in_specs=[pl.BlockSpec(memory_space=pltpu.SMEM)] + vmem(8),
        out_specs=tuple(vmem(4)),
        scratch_shapes=[
            pltpu.VMEM((levels,) + first_shape[1:], jnp.float32),
            pltpu.VMEM(packed.shape, jnp.float32),
            pltpu.VMEM(packed.shape, jnp.float32),
        ],
        compiler_params=params(8),
        name="window",
    )(level_map, received, inner, outer, static_control, static_scale, coefs, obs_weight, innovation)
    incoming = swapped(send)
    inner, outer = exchanged_pairs(inner, outer)

    return pl.pallas_call(
        member_update_kernel,
        out_shape=(array(*ens_control.shape), array(*static_control.shape)),
        in_specs=vmem(10),
        out_specs=tuple(vmem(2)),
        scratch_shapes=[pltpu.VMEM(ens_control.shape[1:], jnp.float32)],
        compiler_params=params(8),
        name="member_update",
    )(
        loc_lat, loc_lon, ens_perts, incoming, ens_control,
        inner, outer, tile_grad, static_control, static_scale,
    )


def exchanged(block, axis):
    count = lax.axis_size("tile")
    forward = [(i, i + 1) for i in range(count - 1)]
    backward = [(target, source) for source, target in forward]
    last = block.shape[axis] - 1
    low = lax.ppermute(lax.slice_in_dim(block, last, last + 1, axis=axis), "tile", forward)
    high = lax.ppermute(lax.slice_in_dim(block, 0, 1, axis=axis), "tile", backward)
    return jnp.concatenate([low, block, high], axis=axis)


def forward_step(state, coeffs):
    padded = exchanged(state, 1)
    return (
        state
        + coeffs[0] * (padded[:, 2:] - state)
        + coeffs[1] * (padded[:, :-2] - state)
        + coeffs[2] * (jnp.roll(state, -1, 2) - state)
        + coeffs[3] * (jnp.roll(state, 1, 2) - state)
    )


def adjoint_step(adjoint, coeffs):
    coef_sum = coeffs[0] + coeffs[1] + coeffs[2] + coeffs[3]
    padded = exchanged(jnp.stack([coeffs[0] * adjoint, coeffs[1] * adjoint]), 2)
    return (
        (1.0 - coef_sum) * adjoint
        + padded[0][:, :-2]
        + padded[1][:, 2:]
        + jnp.roll(coeffs[2] * adjoint, 1, 2)
        + jnp.roll(coeffs[3] * adjoint, -1, 2)
    )


def any_local(
    level_map, loc_lat, loc_lon, ens_perts, ens_control,
    static_control, static_scale, coefs, obs_weight, innovation,
):
    tiles = lax.axis_size("tile")
    level_ids = jnp.arange(static_control.shape[0], dtype=jnp.int32)
    level_onehot = (level_map[:, None] == level_ids[None, :]).astype(jnp.float32)
    lat_smoothed = jnp.einsum(
        "ij,bjk->bik", loc_lat, ens_control.astype(jnp.bfloat16),
        preferred_element_type=jnp.float32,
    ).astype(jnp.bfloat16)
    member_field = jnp.einsum(
        "bij,kj->bik", lat_smoothed, loc_lon, preferred_element_type=jnp.float32
    )
    partial_value = jnp.sum(ens_perts.astype(jnp.float32) * member_field, axis=0)
    pieces = partial_value.reshape(tiles, -1, partial_value.shape[1])
    received = lax.all_to_all(pieces, "tile", split_axis=0, concat_axis=0, tiled=True)
    ens_incr = jnp.einsum("dl,dij->lij", level_onehot, received, precision=lax.Precision.HIGHEST)
    state = static_scale * static_control + ens_incr
    weighted = []
    for section in range(STEPS):
        state = forward_step(state, coefs)
        weighted.append(obs_weight[section] * (state - innovation[section]))
    adjoint = weighted[STEPS - 1]
    for section in range(STEPS - 2, -1, -1):
        adjoint = adjoint_step(adjoint, coefs) + weighted[section]
    gradient = adjoint_step(adjoint, coefs)
    static_final = static_control - STEP_SIZE * (static_control + static_scale * gradient)
    outgoing = jnp.take(gradient, level_map, axis=0)
    incoming = lax.all_to_all(outgoing, "tile", split_axis=0, concat_axis=0, tiled=True)
    grad_field = incoming.reshape(-1, incoming.shape[2])
    weighted_grad = (ens_perts.astype(jnp.float32) * grad_field[None]).astype(jnp.bfloat16)
    adjoint_lat = jnp.einsum(
        "ji,bjk->bik", loc_lat, weighted_grad, preferred_element_type=jnp.float32
    ).astype(jnp.bfloat16)
    member_grad = jnp.einsum("bij,jk->bik", adjoint_lat, loc_lon, preferred_element_type=jnp.float32)
    return ens_control - STEP_SIZE * (ens_control + member_grad), static_final


def local(*args):
    levels, rows, nlon = args[5].shape
    whole = rows % SUB == 0 and nlon % LANES == 0 and levels % GROUP == 0
    return (whole_local if whole else any_local)(*args)


def solution(mesh):
    in_specs = (
        P(),
        P(),
        P(),
        P(("groups", "tile"), None, None),
        P(("groups", "tile"), None, None),
        P("groups", "tile", None),
        P("groups", "tile", None),
        P(None, "groups", "tile", None),
        P(None, "groups", "tile", None),
        P(None, "groups", "tile", None),
    )
    out_specs = (P(("groups", "tile"), None, None), P("groups", "tile", None))
    return jax.shard_map(local, mesh=mesh, in_specs=in_specs, out_specs=out_specs, check_vma=False)
```
